128 devices in a mesh: dp: 2 (over core), tensor: 4 (over y), context: 16 (over z, x).
Axes of the slice: x: 4, y: 4, z: 4, core: 2. Of those that a mesh axis runs over, the one named last changes fastest.
Arguments:
- ssm_input: bfloat16 [2, 4096, 4096], P('dp', 'context', 'tensor'), may hold values from -6 to 6
- gate_input: bfloat16 [2, 4096, 4096], P('dp', 'context', 'tensor'), may hold values from -6 to 6
- state_keys: bfloat16 [2, 4096, 1024], P('dp', 'context', 'tensor'), may hold values from -0.3984375 to 0.3984375
- state_queries: bfloat16 [2, 4096, 1024], P('dp', 'context', 'tensor'), may hold values from -0.3984375 to 0.3984375
- step_raw: float32 [2, 64, 4096], P('dp', 'tensor', 'context'), may hold values from -1 to 1.5
- rate_log: float32 [64], P('tensor'), may hold values from -13 to -2, as said below
- skip_gain: float32 [64], P('tensor'), may hold values from 0.5 to 2
- norm_gain: float32 [4096], P('tensor'), may hold values from 0.1 to 1.9
- out_weight: bfloat16 [4096, 4096], P(None, 'tensor'), may hold values from -0.09375 to 0.09375
- out_grad: bfloat16 [2, 4096, 4096], P('dp', 'context', 'tensor'), may hold values from -6 to 6
Outputs:
- grad_input: bfloat16 [2, 4096, 4096], P('dp', 'context', 'tensor')
- grad_gate: bfloat16 [2, 4096, 4096], P('dp', 'context', 'tensor')
- grad_keys: float32 [2, 4096, 1024], P('dp', 'context', 'tensor')
- grad_queries: float32 [2, 4096, 1024], P('dp', 'context', 'tensor')
- grad_step: float32 [2, 64, 4096], P('dp', 'tensor', 'context')
- grad_rate: float32 [64], P('tensor')
- grad_skip: float32 [64], P('tensor')
- grad_norm: float32 [4096], P('tensor')
- grad_weight: float32 [4096, 4096], P(('dp', 'context'), 'tensor')
The draws below stay inside these ranges and needn't reach their ends.
Inputs may be any that keep to these rules, and one draw needn't show every extreme that they name: exp(rate_log) lies between 0.2 / 4096 and 1 / 12.
All inputs are finite; a program needn't handle non-finite values.
Results may differ from the reference program's by a relative error of at most 0.0029.
Values may be sent and summed in bfloat16 or wider, within the bound.
A program may use at most 128 MiB of HBM per device.

```python
import jax
import jax.numpy as jnp
from jax import lax

D = 4096
HEADS = 64
HEAD_DIM = 64
STATE = 128
GROUPS = 8
STRETCH = 256
ROLLOUTS = 2
LENGTH = 4096
INNER = 4096


def draw_rate_log(key, part):
    pick_key, slow_key, fast_key = jax.random.split(jax.random.fold_in(key, 17), 3)
    slow_share = 0.5
    chosen = jax.random.uniform(pick_key, (HEADS,), jnp.float32) < slow_share
    slow_lo = jnp.log(0.2 / LENGTH)
    slow_hi = jnp.log(1.5 / LENGTH)
    slow_vals = jax.random.uniform(slow_key, (HEADS,), jnp.float32, slow_lo, slow_hi)
    fast_vals = jax.random.uniform(fast_key, (HEADS,), jnp.float32, jnp.log(1.0 / 50.0), jnp.log(1.0 / 12.0))
    return jnp.where(chosen, slow_vals, fast_vals).astype(jnp.float32)


def spiked(array, own_key, source, target, shards_of, factor):
    owner, partner = [(jnp.arange(array.shape[axis_at]) // (array.shape[axis_at] // shards_of)).reshape([-1 if axis == axis_at else 1 for axis in range(array.ndim)]) for axis_at in (source, target)]
    chosen = jax.random.permutation(own_key, shards_of)[partner]
    strong = (owner == chosen) | (owner == (partner + shards_of // 2) % shards_of)
    return jnp.where(strong, factor * array, array)


def levels(key, shape, cuts, least, top_value):
    level, own = 1.0, jax.random.fold_in(key, 6)
    for axis_at, blocks in cuts:
        heights = jnp.exp(jax.random.uniform(jax.random.fold_in(own, axis_at), (blocks,), jnp.float32, least / len(cuts), top_value / len(cuts)))
        level = level * jnp.repeat(heights, shape[axis_at] // blocks).reshape([-1 if axis == axis_at else 1 for axis in range(len(shape))])
    return level


def gaussian(rng, shape, deviation, reach, cuts=(), held_as=jnp.bfloat16):
    level = levels(rng, shape, cuts, -0.22, 0.18) if cuts else 1.0
    result = jax.random.normal(rng, shape, jnp.float32) * deviation * level
    return jnp.minimum(jnp.maximum(result, -reach), reach).astype(held_as)


def heavy_noise(rng, extent, width, bound, cuts, heavy, dtype=jnp.bfloat16):
    array = width * jax.random.normal(rng, extent, jnp.float32)
    if cuts:
        array = array * levels(rng, extent, cuts, -0.22, 0.18)
    return jnp.clip(spiked(array, jax.random.fold_in(rng, 3), *heavy), -bound, bound).astype(dtype)


def setup_inputs(seed: int = 0) -> dict:
    key_list = jax.random.split(jax.random.key(seed), 11)
    ssm_input = gaussian(key_list[0], (ROLLOUTS, LENGTH, INNER), 1.0, 6.0, ((0, 2), (1, 16), (2, 4)))
    gate_input = gaussian(key_list[1], (ROLLOUTS, LENGTH, INNER), 1.0, 6.0, ((0, 2), (1, 16), (2, 4)))
    state_keys = gaussian(key_list[2], (ROLLOUTS, LENGTH, GROUPS * STATE), 0.06, 0.3984375, ((0, 2), (1, 16), (2, 4)))
    state_queries = gaussian(key_list[3], (ROLLOUTS, LENGTH, GROUPS * STATE), 0.06, 0.3984375, ((0, 2), (1, 16), (2, 4)))
    step_raw = jnp.clip(-1.0 + 2.5 * jax.random.uniform(key_list[4], (ROLLOUTS, HEADS, LENGTH), jnp.float32) ** levels(key_list[4], (ROLLOUTS, HEADS, LENGTH), ((0, 2), (1, 4), (2, 16)), -0.2, 0.2), -1.0, 1.5)
    rate_log = draw_rate_log(jax.random.fold_in(key_list[10], 71), 0)
    skip_gain = jnp.clip(0.5 + 1.5 * jax.random.uniform(key_list[6], (HEADS,), jnp.float32) ** levels(key_list[6], (HEADS,), ((0, 4),), -0.2, 0.2), 0.5, 2.0)
    norm_gain = jnp.clip(1.0 + 0.18 * jax.random.normal(key_list[7], (INNER,), jnp.float32), 0.1, 1.9)
    out_weight = gaussian(key_list[8], (D, INNER), INNER ** -0.5, 0.09375, ((1, 4),))
    out_grad = heavy_noise(key_list[9], (ROLLOUTS, LENGTH, D), 1.0, 6.0, ((0, 2), (1, 16), (2, 4)), (1, 2, 16, 2.0))
    return dict(ssm_input=ssm_input, gate_input=gate_input, state_keys=state_keys, state_queries=state_queries, step_raw=step_raw, rate_log=rate_log, skip_gain=skip_gain, norm_gain=norm_gain, out_weight=out_weight, out_grad=out_grad)


EPSILON = 1e-05
HIGHEST = lax.Precision.HIGHEST

def decay_terms(step_raw, rate_log, stretch_count):
    step_size = jax.nn.softplus(step_raw).T.reshape(stretch_count, STRETCH, -1)
    cumulative = jnp.cumsum(-jnp.exp(rate_log)[None, None, :] * step_size, axis=1)
    return (step_size, cumulative)

def stretch_states(inputs, key_rows, step_size, cumulative):
    stretch_count, stretch_len, head_count, head_width = inputs.shape
    group_count = key_rows.shape[2]
    weights = jnp.exp(cumulative[:, -1:, :] - cumulative) * step_size
    weighted = (inputs * weights[..., None]).reshape(stretch_count, stretch_len, group_count, head_count // group_count, head_width)
    local_states = jnp.einsum('kqgep,kqgn->kgepn', weighted, key_rows, precision=HIGHEST)
    return (local_states.reshape(stretch_count, head_count, head_width, key_rows.shape[3]), cumulative[:, -1, :])

def chain_states(local_states, stretch_totals, initial):

    def advance(carried, pieces):
        return (jnp.exp(pieces[1])[:, None, None] * carried + pieces[0], carried)
    leaving, entering = lax.scan(advance, initial, (local_states, stretch_totals))
    return (entering, leaving)

def stretch_output(pieces):
    inputs, key_rows, query_rows, step_size, cumulative, entering = pieces
    stretch_len, head_count, head_width = inputs.shape
    group_count = key_rows.shape[1]
    per_group = head_count // group_count
    scores = jnp.einsum('ign,jgn->gij', query_rows, key_rows, precision=HIGHEST)
    row_index = lax.broadcasted_iota(jnp.int32, (stretch_len, stretch_len), 0)
    col_index = lax.broadcasted_iota(jnp.int32, (stretch_len, stretch_len), 1)
    causal = (row_index >= col_index)[None]
    by_head = cumulative.T
    spread_log = by_head[:, :, None] - by_head[:, None, :]
    mixing = jnp.where(causal, jnp.exp(jnp.where(causal, spread_log, 0.0)), 0.0) * step_size.T[:, None, :]
    mixing = mixing.reshape(group_count, per_group, stretch_len, stretch_len) * scores[:, None]
    grouped = inputs.reshape(stretch_len, group_count, per_group, head_width)
    within = jnp.einsum('geij,jgep->igep', mixing, grouped, precision=HIGHEST).reshape(stretch_len, head_count, head_width)
    states = entering.reshape(group_count, per_group, head_width, -1)
    carried = jnp.einsum('ign,gepn->igep', query_rows, states, precision=HIGHEST).reshape(stretch_len, head_count, head_width)
    return within + jnp.exp(cumulative)[:, :, None] * carried

def run_forward(inputs, key_rows, query_rows, step_raw, rate_log, skip_gain, initial):
    stretch_count = inputs.shape[0]
    step_size, cumulative = decay_terms(step_raw, rate_log, stretch_count)
    local_states, stretch_totals = stretch_states(inputs, key_rows, step_size, cumulative)
    entering, leaving = chain_states(local_states, stretch_totals, initial)
    outputs = lax.map(jax.checkpoint(stretch_output), (inputs, key_rows, query_rows, step_size, cumulative, entering))
    outputs = outputs + skip_gain[None, None, :, None] * inputs
    return outputs.reshape(stretch_count * inputs.shape[1], -1)

def norm_gate(ssd_out, gate_vals, norm_gain):
    gated = ssd_out * jax.nn.silu(gate_vals)
    row_count, channels = gated.shape
    group_width = HEADS // GROUPS * HEAD_DIM
    grouped = gated.reshape(row_count, channels // group_width, group_width)
    inverse = lax.rsqrt(lax.optimization_barrier(jnp.mean(grouped * grouped, axis=-1, keepdims=True)) + EPSILON)
    return (grouped * inverse).reshape(row_count, channels) * norm_gain

def to_stretches(matrix, stretch_count, inner_width):
    return matrix.astype(jnp.float32).reshape(stretch_count, STRETCH, -1, inner_width)

def reference(ssm_input, gate_input, state_keys, state_queries, step_raw, rate_log, skip_gain, norm_gain, out_weight, out_grad):
    row_count = ssm_input.shape[1]
    stretch_count = row_count // STRETCH
    initial = jnp.zeros((HEADS, HEAD_DIM, STATE), jnp.float32)
    grad_weight = jnp.zeros(out_weight.shape, jnp.float32)
    grad_rate = jnp.zeros((HEADS,), jnp.float32)
    grad_skip = jnp.zeros((HEADS,), jnp.float32)
    grad_norm = jnp.zeros(norm_gain.shape, jnp.float32)
    input_list, gate_list, keys_list, query_list, step_list = ([], [], [], [], [])
    for rollout in range(ssm_input.shape[0]):
        inputs = to_stretches(ssm_input[rollout], stretch_count, HEAD_DIM)
        key_rows = to_stretches(state_keys[rollout], stretch_count, STATE)
        query_rows = to_stretches(state_queries[rollout], stretch_count, STATE)
        ssd_out, pull_ssd = jax.vjp(run_forward, inputs, key_rows, query_rows, step_raw[rollout], rate_log, skip_gain, initial)
        normed, pull_norm = jax.vjp(norm_gate, ssd_out, gate_input[rollout].astype(jnp.float32), norm_gain)
        normed = normed.astype(jnp.bfloat16)
        grad_normed = jnp.dot(out_grad[rollout], out_weight, preferred_element_type=jnp.float32)
        grad_weight = grad_weight + lax.dot_general(out_grad[rollout], normed, (((0,), (0,)), ((), ())), preferred_element_type=jnp.float32)
        grad_ssd, gate_part, norm_part = pull_norm(grad_normed)
        ssd_grads = pull_ssd(grad_ssd)
        input_list.append(ssd_grads[0].reshape(row_count, -1).astype(jnp.bfloat16))
        gate_list.append(gate_part.astype(jnp.bfloat16))
        keys_list.append(ssd_grads[1].reshape(row_count, -1))
        query_list.append(ssd_grads[2].reshape(row_count, -1))
        step_list.append(ssd_grads[3])
        grad_rate = grad_rate + ssd_grads[4]
        grad_skip = grad_skip + ssd_grads[5]
        grad_norm = grad_norm + norm_part
    return (jnp.stack(input_list), jnp.stack(gate_list), jnp.stack(keys_list), jnp.stack(query_list), jnp.stack(step_list), grad_rate, grad_skip, grad_norm, grad_weight)
```

```python
import jax
import jax.numpy as jnp
from jax import lax
from jax.experimental import pallas as pl
from jax.experimental.pallas import tpu as pltpu
from jax.sharding import PartitionSpec as P

F32 = jnp.float32
BF = jnp.bfloat16
EPSILON = 1e-05
MESH = pl.DeviceIdType.MESH

T = 256
C = 1024
NH = 16
NQ = 8
W = 128
CTX = 16


def dot(a, b):
    return lax.dot_general(a, b, (((1,), (0,)), ((), ())), preferred_element_type=F32)


def dot_t(a, b):
    return lax.dot_general(a, b, (((1,), (1,)), ((), ())), preferred_element_type=F32)


def tdot(a, b):
    return lax.dot_general(a, b, (((0,), (0,)), ((), ())), preferred_element_type=F32)


def split2(v):
    hi = v.astype(BF)
    return hi, (v - hi.astype(F32)).astype(BF)


def split3(v):
    hi = v.astype(BF)
    rest = v - hi.astype(F32)
    mid = rest.astype(BF)
    return hi, mid, (rest - mid.astype(F32)).astype(BF)


def dot3(v, ones):
    parts = dot(jnp.concatenate(split3(v), axis=0), ones)
    return parts[0:NH] + parts[NH : 2 * NH] + parts[2 * NH : 3 * NH]


def iota(shape, axis):
    return lax.broadcasted_iota(jnp.int32, shape, axis)


def lanes(q):
    return pl.ds(pl.multiple_of(q * W, W), W)


def per_head(row):
    own = (iota((NH, C), 1) // 64) == iota((NH, C), 0)
    return jnp.sum(jnp.where(own, row, 0.0), axis=1, keepdims=True)


def kernel(
    x_ref, k_ref, q_ref, step_ref, rate_ref, skip_ref, gain_ref, gate_hbm, w_hbm, og_hbm,
    gi_hbm, gg_hbm, gk_hbm, gq_hbm, gs_hbm, sm_hbm, gw_hbm,
    gate_v, w_v, ogf, ogp, ogt, nm2,
    cumx, eexp, wexp, cum_s, stp_s, kt, qt, k2, q2, sc,
    snd, rcv, ent_s, ent, bsnd, brcv, out_s, outb,
    mt, phi, plo, y_s, gn_s, ga_s, g_s, acc, acc2, invb, mub,
    ds_s, dxw, dq_s, dk_s, rows, accr, accc, accv,
    gi_v, gg_v, gs_v, sm_own, sm_rcv, sm_sum, sm_p,
    sa, sb, owna, ownb, ra, rb, s2a, s2b, r2a, r2b, gw_v,
    in_sem, out_sem, og_ss, og_rs, fa_ss, fa_rs, fb_ss, fb_rs, ba_ss, ba_rs, bb_ss, bb_rs,
    p_ss, p_rs, r1_ss, r1_rs, r2_ss, r2_rs, m_ss, m_rs,
):
    me = lax.axis_index("context")
    myt = lax.axis_index("tensor")
    mydp = lax.axis_index("dp")
    mz, mx = me // 4, me % 4
    other = 1 - mydp
    right, left = (myt + 1) % 4, (myt + 3) % 4

    barrier = pltpu.get_barrier_semaphore()

    def greet(off, carry):
        pl.semaphore_signal(
            barrier, inc=1, device_id={"context": (me + off) % CTX}, device_id_type=MESH
        )
        return carry

    lax.fori_loop(1, CTX, greet, 0)
    pl.semaphore_signal(barrier, inc=1, device_id={"tensor": right}, device_id_type=MESH)
    pl.semaphore_signal(barrier, inc=1, device_id={"tensor": left}, device_id_type=MESH)
    pl.semaphore_signal(barrier, inc=1, device_id={"dp": other}, device_id_type=MESH)

    in_og = pltpu.make_async_copy(og_hbm, ogf.at[myt], in_sem.at[0])
    in_gate = pltpu.make_async_copy(gate_hbm, gate_v, in_sem.at[1])
    in_w = pltpu.make_async_copy(w_hbm, w_v, in_sem.at[2])
    in_og.start()
    in_gate.start()
    in_w.start()

    raw = step_ref[...]
    eye = iota((NH, NH), 0) == iota((NH, NH), 1)
    slope = jnp.sum(jnp.where(eye, jnp.exp(rate_ref[...]), 0.0), axis=1, keepdims=True)
    step = jnp.maximum(raw, 0.0) + jnp.log(1.0 + jnp.exp(-jnp.abs(raw)))
    decay = -slope * step
    upper = (iota((T, T), 0) <= iota((T, T), 1)).astype(BF)
    cum = dot3(decay, upper)
    total = cum[:, T - 1 : T]
    stp_s[...] = step
    cum_s[...] = cum
    spread = ((iota((3 * NH, C), 0) % NH) == (iota((3 * NH, C), 1) // 64)).astype(BF)

    def expand(v, to):
        pieces = jnp.concatenate(split3(v), axis=0).astype(F32)
        turned = jnp.concatenate([pieces, jnp.zeros((W - 3 * NH, T), F32)], axis=0).T
        to[...] = dot(turned[:, : 3 * NH].astype(BF), spread)

    expand(jnp.exp(cum), eexp)
    expand(jnp.exp(total - cum) * step, wexp)
    expand(cum, cumx)
    own = (iota((NH, C), 1) // 64) == iota((NH, C), 0)
    skip_col = jnp.sum(jnp.where(eye, skip_ref[...], 0.0), axis=1, keepdims=True)
    rows[3] = jnp.sum(jnp.where(own, skip_col, 0.0), axis=0, keepdims=True)

    for g in range(2):
        kg = k_ref[:, g * W : (g + 1) * W]
        qg = q_ref[:, g * W : (g + 1) * W]
        kt[g] = kg.T
        qt[g] = qg.T
        k2[g] = jnp.concatenate([kg, kg], axis=1)
        q2[g] = jnp.concatenate([qg, qg], axis=1)

    def local_state(q, carry):
        hi, lo = split2(x_ref[:, lanes(q)].astype(F32) * wexp[:, lanes(q)])
        both = dot(kt[q // 4], jnp.concatenate([hi, lo], axis=1))
        state = both[:, :W] + both[:, W:]
        factor = jnp.broadcast_to(eexp[T - 1 : T, lanes(q)], (8, W))
        snd[2 * q, 0:64] = state[0:64]
        snd[2 * q + 1, 0:64] = state[64:]
        snd[2 * q, 64:72] = factor
        snd[2 * q + 1, 64:72] = factor
        return carry

    lax.fori_loop(0, NQ, local_state, 0)

    pl.semaphore_wait(barrier, CTX + 2)

    def ctx_copy(src, dst, ss, rs, peer, src_slot, dst_slot):
        return pltpu.make_async_remote_copy(
            src_ref=src.at[src_slot],
            dst_ref=dst.at[dst_slot],
            send_sem=ss.at[src_slot],
            recv_sem=rs.at[dst_slot],
            device_id={"context": peer},
            device_id_type=MESH,
        )

    def send_all(src, dst, ss, rs):
        def one(off, carry):
            peer = (me + off) % CTX
            ctx_copy(src, dst, ss, rs, peer, peer, me).start()
            return carry

        lax.fori_loop(1, CTX, one, 0)

    def recv_all(src, dst, ss, rs):
        def one(off, carry):
            peer = (me + off) % CTX
            ctx_copy(src, dst, ss, rs, peer, peer, peer).wait_recv()
            return carry

        lax.fori_loop(1, CTX, one, 0)

    def drain_all(src, dst, ss, rs):
        def one(off, carry):
            peer = (me + off) % CTX
            ctx_copy(src, dst, ss, rs, peer, peer, me).wait_send()
            return carry

        lax.fori_loop(1, CTX, one, 0)

    send_all(snd, rcv, fa_ss, fa_rs)

    def ring(src, dst, sem, peer):
        return pltpu.make_async_remote_copy(
            src_ref=src,
            dst_ref=dst,
            send_sem=og_ss.at[sem],
            recv_sem=og_rs.at[sem],
            device_id={"tensor": peer},
            device_id_type=MESH,
        )

    to_right = ring(og_hbm, ogf.at[myt], 0, right)
    to_left = ring(og_hbm, ogf.at[myt], 1, left)
    to_right.start()
    to_left.start()

    for g in range(2):
        sc[g] = dot_t(q_ref[:, g * W : (g + 1) * W], k_ref[:, g * W : (g + 1) * W])
    causal = iota((T, T), 0) >= iota((T, T), 1)
    first = iota((T, W), 1) < 64

    def within(q, carry):
        xp = x_ref[:, lanes(q)]
        spread_tile = cumx[:, lanes(q)]
        outs = []
        for hh in range(2):
            h = 2 * q + hh
            column = spread_tile[:, 64 * hh : 64 * hh + 1]
            gap = column - cum_s[pl.ds(h, 1), :]
            m = jnp.exp(jnp.where(causal, gap, -1e30)) * stp_s[pl.ds(h, 1), :]
            mt[h] = m
            hi, lo = split2(m * sc[q // 4])
            phi[h] = hi
            plo[h] = lo
            outs.append(dot(hi, xp) + dot(lo, xp))
        y_s[:, lanes(q)] = jnp.where(first, outs[0], outs[1])
        return carry

    lax.fori_loop(0, NQ, within, 0)

    rcv[me] = snd[me]
    recv_all(snd, rcv, fa_ss, fa_rs)
    run = jnp.zeros((64, W), F32)
    for s in range(CTX):
        ent_s[s] = run
        run = rcv[s, 64:65, :] * run + rcv[s, 0:64, :]
    send_all(ent_s, ent, fb_ss, fb_rs)
    ent[me] = ent_s[me]

    in_og.wait()
    to_right.wait_recv()
    relay_right = ring(ogf.at[left, 0:128], ogf.at[left, 0:128], 2, right)
    relay_right.start()
    to_left.wait_recv()
    relay_left = ring(ogf.at[right, 128:256], ogf.at[right, 128:256], 3, left)
    relay_left.start()
    in_w.wait()

    def project(chunk, first_term):
        def one(n, carry):
            part = dot(
                ogf[chunk], w_v[pl.ds(pl.multiple_of(chunk * C, C), C), pl.ds(pl.multiple_of(n * 256, 256), 256)]
            )
            where = pl.ds(pl.multiple_of(n * 256, 256), 256)
            gn_s[:, where] = part if first_term else gn_s[:, where] + part
            return carry

        lax.fori_loop(0, 4, one, 0)

    project(myt, True)
    project(left, False)
    project(right, False)
    relay_right.wait_recv()
    relay_left.wait_recv()

    def pair(src, dst, sem):
        return pltpu.make_async_remote_copy(
            src_ref=src,
            dst_ref=dst,
            send_sem=p_ss.at[sem],
            recv_sem=p_rs.at[sem],
            device_id={"dp": other},
            device_id_type=MESH,
        )

    pair_og = [pair(ogf.at[2 * other + i], ogp.at[i], i) for i in range(2)]
    for copy in pair_og:
        copy.start()
    project((myt + 2) % 4, False)

    def turn_own(i, carry):
        at = pl.ds(pl.multiple_of(i * W, W), W)
        ogt[at, 0:T] = ogf[2 * mydp + i // 8, :, lanes(i % 8)].T
        return carry

    lax.fori_loop(0, 16, turn_own, 0)
    for copy in pair_og:
        copy.wait_recv()

    def turn_pair(i, carry):
        at = pl.ds(pl.multiple_of(i * W, W), W)
        ogt[at, T : 2 * T] = ogp[i // 8, :, lanes(i % 8)].T
        return carry

    lax.fori_loop(0, 16, turn_pair, 0)
    in_gate.wait()
    recv_all(ent_s, ent, fb_ss, fb_rs)

    acc[...] = jnp.zeros_like(acc)
    acc2[...] = jnp.zeros_like(acc2)

    def entering(q):
        return jnp.concatenate([ent[2 * q], ent[2 * q + 1]], axis=0)

    def scan_out(q, carry):
        g = q // 4
        carried = dot(q2[g], jnp.concatenate(split2(entering(q)), axis=0))
        y = y_s[:, lanes(q)] + eexp[:, lanes(q)] * carried
        y_s[:, lanes(q)] = y
        ssd = y + rows[3, :, lanes(q)] * x_ref[:, lanes(q)].astype(F32)
        gate = gate_v[:, lanes(q)].astype(F32)
        gated = ssd * (gate / (1.0 + jnp.exp(-gate)))
        ga_s[:, lanes(q)] = gated
        acc[g] += gated * gated
        acc2[g] += gn_s[:, lanes(q)] * gain_ref[:, lanes(q)] * gated
        return carry

    lax.fori_loop(0, NQ, scan_out, 0)
    for g in range(2):
        mean = jnp.sum(acc[g], axis=1, keepdims=True) * (1.0 / 512)
        inverse = lax.rsqrt(mean + EPSILON)
        shift = jnp.sum(acc2[g], axis=1, keepdims=True) * (1.0 / 512)
        invb[g] = jnp.broadcast_to(inverse, (T, W))
        mub[g] = jnp.broadcast_to(shift * inverse * inverse, (T, W))

    def normalize(q, carry):
        value = ga_s[:, lanes(q)] * invb[q // 4] * gain_ref[:, lanes(q)]
        nm2[0:T, lanes(q)] = value.astype(BF)
        return carry

    lax.fori_loop(0, NQ, normalize, 0)
    pair_nm = pair(nm2.at[0:T], nm2.at[T : 2 * T], 2)
    pair_nm.start()

    def norm_back(q, carry):
        g = q // 4
        gated = ga_s[:, lanes(q)]
        inverse = invb[g]
        gn = gn_s[:, lanes(q)]
        d_gated = inverse * (gn * gain_ref[:, lanes(q)] - gated * mub[g])
        rows[0, :, lanes(q)] = jnp.sum(gn * gated * inverse, axis=0, keepdims=True)
        gate = gate_v[:, lanes(q)].astype(F32)
        xv = x_ref[:, lanes(q)].astype(F32)
        sig = 1.0 / (1.0 + jnp.exp(-gate))
        silu = gate * sig
        y = y_s[:, lanes(q)]
        ssd = y + rows[3, :, lanes(q)] * xv
        gg_v[:, lanes(q)] = (d_gated * ssd * (sig * (1.0 + gate - silu))).astype(BF)
        grad = d_gated * silu
        g_s[:, lanes(q)] = grad
        rows[1, :, lanes(q)] = jnp.sum(grad * xv, axis=0, keepdims=True)
        hi, lo = split2(eexp[:, lanes(q)] * grad)
        both = dot(qt[g], jnp.concatenate([hi, lo], axis=1))
        into = both[:, :W] + both[:, W:]
        bsnd[2 * q] = into[0:64]
        bsnd[2 * q + 1] = into[64:]
        return carry

    lax.fori_loop(0, NQ, norm_back, 0)
    out_gg = pltpu.make_async_copy(gg_v, gg_hbm, out_sem.at[0])
    out_gg.start()
    send_all(bsnd, brcv, ba_ss, ba_rs)

    pair_nm.wait_recv()

    def weight_block(block, half):
        at = pl.ds(pl.multiple_of(block * W, W), W)
        return dot(ogt[at, :], nm2[:, half * 512 : half * 512 + 512])

    def phase1(src, dst, sem, peer):
        return pltpu.make_async_remote_copy(
            src_ref=src,
            dst_ref=dst,
            send_sem=r1_ss.at[sem],
            recv_sem=r1_rs.at[sem],
            device_id={"context": peer},
            device_id_type=MESH,
        )

    def phase2(src, dst, sem, peer):
        return pltpu.make_async_remote_copy(
            src_ref=src,
            dst_ref=dst,
            send_sem=r2_ss.at[sem],
            recv_sem=r2_rs.at[sem],
            device_id={"context": peer},
            device_id_type=MESH,
        )

    sends1 = []
    for d in (2, 1, 3):
        px = (mx + d) % 4
        pz = (mz + d) % 4

        def fill_a(i, carry, px=px, d=d):
            sa[d - 1, i] = weight_block(i * 4 + px, 0).astype(BF)
            return carry

        lax.fori_loop(0, 4, fill_a, 0)
        copy = phase1(sa.at[d - 1], ra.at[d - 1], d - 1, mz * 4 + px)
        copy.start()
        sends1.append(copy)

        def fill_b(i, carry, pz=pz, d=d):
            sb[d - 1, i] = weight_block(pz * 4 + i, 1).astype(BF)
            return carry

        lax.fori_loop(0, 4, fill_b, 0)
        copy = phase1(sb.at[d - 1], rb.at[d - 1], 3 + d - 1, pz * 4 + mx)
        copy.start()
        sends1.append(copy)

    def fill_own(i, carry):
        owna[i] = weight_block(i * 4 + mx, 0)
        ownb[i] = weight_block(mz * 4 + i, 1)
        return carry

    lax.fori_loop(0, 4, fill_own, 0)

    brcv[me] = bsnd[me]
    recv_all(bsnd, brcv, ba_ss, ba_rs)
    run = jnp.zeros((64, W), F32)
    for s in range(CTX - 1, -1, -1):
        out_s[s] = run
        run = brcv[s] + rcv[s, 64:65, :] * run
    send_all(out_s, outb, bb_ss, bb_rs)
    outb[me] = out_s[me]

    ds_s[...] = jnp.zeros_like(ds_s)
    dq_s[...] = jnp.zeros_like(dq_s)
    dk_s[...] = jnp.zeros_like(dk_s)
    accr[...] = jnp.zeros_like(accr)
    accc[...] = jnp.zeros_like(accc)
    accv[...] = jnp.zeros_like(accv)

    def head_sums(q, value):
        row, lane = iota((NH, 2 * W), 0), iota((NH, 2 * W), 1) % W
        pick = (row == 2 * q + lane // 64).astype(BF)
        return dot_t(pick, jnp.concatenate(split2(value), axis=1))

    def within_back(q, carry):
        g = q // 4
        xp = x_ref[:, lanes(q)]
        grad = g_s[:, lanes(q)]
        ghi, glo = split2(grad)
        gthi, gtlo = ghi.T, glo.T
        x2 = jnp.concatenate([xp, xp], axis=1)
        zero = jnp.zeros((T, W), BF)
        parts = []
        total_ds = ds_s[g]
        for hh in range(2):
            h = 2 * q + hh
            keep = first if hh == 0 else jnp.logical_not(first)
            g2 = jnp.concatenate([jnp.where(keep, ghi, zero), jnp.where(keep, glo, zero)], axis=1)
            total_ds = total_ds + dot_t(g2, x2) * mt[h]
            a, b = gthi[64 * hh : 64 * hh + 64], gtlo[64 * hh : 64 * hh + 64]
            both = dot(jnp.concatenate([a, b], axis=0), phi[h])
            parts.append(both[0:64] + both[64:] + dot(a, plo[h]))
        ds_s[g] = total_ds
        dxw[:, lanes(q)] = jnp.concatenate(parts, axis=0).T
        accr[...] += head_sums(q, grad * y_s[:, lanes(q)])
        ehi, elo = split2(eexp[:, lanes(q)] * grad)
        shi, slo = split2(entering(q))
        to_q = dot_t(jnp.concatenate([ehi, elo], axis=1), jnp.concatenate([shi, shi], axis=1))
        dq_s[:, lanes(g)] += to_q + dot_t(ehi, slo)
        return carry

    lax.fori_loop(0, NQ, within_back, 0)
    for g in range(2):
        hi, lo = split2(ds_s[g])
        kg = k_ref[:, g * W : (g + 1) * W]
        qg = q_ref[:, g * W : (g + 1) * W]
        dq_s[:, g * W : (g + 1) * W] += dot(hi, kg) + dot(lo, kg)
        dk_s[:, g * W : (g + 1) * W] = tdot(hi, qg) + tdot(lo, qg)
    out_gq = pltpu.make_async_copy(dq_s, gq_hbm, out_sem.at[1])
    out_gq.start()

    recv_all(out_s, outb, bb_ss, bb_rs)

    def state_back(q, carry):
        g = q // 4
        d_state = jnp.concatenate([outb[2 * q], outb[2 * q + 1]], axis=0)
        dhi, dlo = split2(d_state)
        rows[2, :, lanes(q)] = jnp.sum(d_state * entering(q), axis=0, keepdims=True)
        weight = wexp[:, lanes(q)]
        xv = x_ref[:, lanes(q)].astype(F32)
        via = weight * dot(k2[g], jnp.concatenate([dhi, dlo], axis=0))
        dx = dxw[:, lanes(q)] + via
        gi_v[:, lanes(q)] = (dx + rows[3, :, lanes(q)] * g_s[:, lanes(q)]).astype(BF)
        accc[...] += head_sums(q, xv * dx)
        accv[...] += head_sums(q, xv * via)
        whi, wlo = split2(weight * xv)
        to_k = dot_t(jnp.concatenate([whi, wlo], axis=1), jnp.concatenate([dhi, dhi], axis=1))
        dk_s[:, lanes(g)] += to_k + dot_t(whi, dlo)
        return carry

    lax.fori_loop(0, NQ, state_back, 0)
    out_gi = pltpu.make_async_copy(gi_v, gi_hbm, out_sem.at[2])
    out_gi.start()
    out_gk = pltpu.make_async_copy(dk_s, gk_hbm, out_sem.at[3])
    out_gk.start()

    raw = step_ref[...]
    slope = jnp.sum(jnp.where(eye, jnp.exp(rate_ref[...]), 0.0), axis=1, keepdims=True)
    step = stp_s[...]
    lower = (iota((T, T), 0) >= iota((T, T), 1)).astype(BF)
    after = dot3(accr[...] - accc[...], lower)
    log_grad = per_head(rows[2] * eexp[T - 1 : T, :])
    d_total = jnp.sum(accv[...], axis=1, keepdims=True) + log_grad
    d_decay = after + d_total
    gs_v[...] = (accc[...] / step - slope * d_decay) / (1.0 + jnp.exp(-raw))
    out_gs = pltpu.make_async_copy(gs_v, gs_hbm, out_sem.at[4])
    out_gs.start()
    rate_part = jnp.sum(d_decay * (-slope * step), axis=1, keepdims=True)
    lane = iota((NH, W), 1)
    sm_own[0:NH] = jnp.where(lane == 0, rate_part, jnp.where(lane == 1, per_head(rows[1]), 0.0))
    for i in range(NQ):
        sm_own[NH + i : NH + i + 1] = rows[0, :, i * W : (i + 1) * W]

    def small_copy(peer, slot):
        return pltpu.make_async_remote_copy(
            src_ref=sm_own,
            dst_ref=sm_rcv.at[slot],
            send_sem=m_ss.at[peer],
            recv_sem=m_rs.at[slot],
            device_id={"context": peer},
            device_id_type=MESH,
        )

    def small_send(off, carry):
        small_copy((me + off) % CTX, me).start()
        return carry

    def small_recv(off, carry):
        small_copy((me + off) % CTX, (me + off) % CTX).wait_recv()
        return carry

    def small_drain(off, carry):
        small_copy((me + off) % CTX, me).wait_send()
        return carry

    lax.fori_loop(1, CTX, small_send, 0)
    sm_rcv[me] = sm_own[...]

    for d in (1, 3, 2):
        phase1(sa.at[d - 1], ra.at[d - 1], d - 1, mz * 4 + mx).wait_recv()
        phase1(sb.at[d - 1], rb.at[d - 1], 3 + d - 1, mz * 4 + mx).wait_recv()

    def sum_a(i):
        value = owna[i]
        for d in range(3):
            value = value + ra[d, i].astype(F32)
        return value

    def sum_b(i):
        value = ownb[i]
        for d in range(3):
            value = value + rb[d, i].astype(F32)
        return value

    sends2 = []
    for d in (2, 1, 3):
        pz = (mz + d) % 4
        px = (mx + d) % 4
        s2a[d - 1] = sum_a(pz).astype(BF)
        copy = phase2(s2a.at[d - 1], r2a.at[d - 1], d - 1, pz * 4 + mx)
        copy.start()
        sends2.append(copy)
        s2b[d - 1] = sum_b(px).astype(BF)
        copy = phase2(s2b.at[d - 1], r2b.at[d - 1], 3 + d - 1, mz * 4 + px)
        copy.start()
        sends2.append(copy)
    gw_v[:, 0:512] = sum_a(mz)
    gw_v[:, 512:1024] = sum_b(mx)

    lax.fori_loop(1, CTX, small_recv, 0)
    value = sm_rcv[0]
    for s in range(1, CTX):
        value = value + sm_rcv[s]
    sm_sum[...] = value
    pair_sm = pair(sm_sum, sm_p, 3)
    pair_sm.start()

    for copy in sends2:
        copy.wait_recv()
    for d in range(3):
        gw_v[:, 0:512] += r2a[d].astype(F32)
        gw_v[:, 512:1024] += r2b[d].astype(F32)
    out_gw = pltpu.make_async_copy(gw_v, gw_hbm, out_sem.at[5])
    out_gw.start()

    pair_sm.wait()
    sm_sum[...] += sm_p[...]
    out_sm = pltpu.make_async_copy(sm_sum, sm_hbm, out_sem.at[6])
    out_sm.start()

    drain_all(snd, rcv, fa_ss, fa_rs)
    drain_all(ent_s, ent, fb_ss, fb_rs)
    drain_all(bsnd, brcv, ba_ss, ba_rs)
    drain_all(out_s, outb, bb_ss, bb_rs)
    lax.fori_loop(1, CTX, small_drain, 0)
    for copy in (to_right, to_left, relay_right, relay_left, *pair_og, pair_nm, *sends1, *sends2):
        copy.wait_send()
    for copy in (out_gg, out_gq, out_gi, out_gk, out_gs, out_gw, out_sm):
        copy.wait()


def body(
    ssm_input, gate_input, state_keys, state_queries, step_raw,
    rate_log, skip_gain, norm_gain, out_weight, out_grad,
):
    vmem, anywhere = pl.BlockSpec(memory_space=pltpu.VMEM), pl.BlockSpec(memory_space=pl.ANY)
    V, S = pltpu.VMEM, pltpu.SemaphoreType.DMA
    scratch = [
        V((T, C), BF), V((4 * C, C), BF), V((4, T, C), BF), V((2, T, C), BF), V((2 * C, 2 * T), BF),
        V((2 * T, C), BF),
        V((T, C), F32), V((T, C), F32), V((T, C), F32), V((NH, T), F32), V((NH, T), F32),
        V((2, W, T), BF), V((2, W, T), BF), V((2, T, 2 * W), BF), V((2, T, 2 * W), BF),
        V((2, T, T), F32),
        V((CTX, 72, W), F32), V((CTX, 72, W), F32), V((CTX, 64, W), F32), V((CTX, 64, W), F32),
        V((CTX, 64, W), F32), V((CTX, 64, W), F32), V((CTX, 64, W), F32), V((CTX, 64, W), F32),
        V((NH, T, T), F32), V((NH, T, T), BF), V((NH, T, T), BF),
        V((T, C), F32), V((T, C), F32), V((T, C), F32), V((T, C), F32),
        V((2, T, W), F32), V((2, T, W), F32), V((2, T, W), F32), V((2, T, W), F32),
        V((2, T, T), F32), V((T, C), F32), V((T, 2 * W), F32), V((T, 2 * W), F32),
        V((4, 1, C), F32), V((NH, T), F32), V((NH, T), F32), V((NH, T), F32),
        V((T, C), BF), V((T, C), BF), V((NH, T), F32),
        V((24, W), F32), V((CTX, 24, W), F32), V((24, W), F32), V((24, W), F32),
        V((3, 4, W, 512), BF), V((3, 4, W, 512), BF), V((4, W, 512), F32), V((4, W, 512), F32),
        V((3, 4, W, 512), BF), V((3, 4, W, 512), BF),
        V((3, W, 512), BF), V((3, W, 512), BF), V((3, W, 512), BF), V((3, W, 512), BF),
        V((W, C), F32),
        S((3,)), S((7,)), S((4,)), S((4,)),
        S((CTX,)), S((CTX,)), S((CTX,)), S((CTX,)), S((CTX,)), S((CTX,)), S((CTX,)), S((CTX,)),
        S((4,)), S((4,)), S((6,)), S((6,)), S((6,)), S((6,)), S((CTX,)), S((CTX,)),
    ]
    gi, gg, gk, gq, gs, sm, gw = pl.pallas_call(
        kernel,
        out_shape=(
            jax.ShapeDtypeStruct((T, C), BF),
            jax.ShapeDtypeStruct((T, C), BF),
            jax.ShapeDtypeStruct((T, 2 * W), F32),
            jax.ShapeDtypeStruct((T, 2 * W), F32),
            jax.ShapeDtypeStruct((NH, T), F32),
            jax.ShapeDtypeStruct((24, W), F32),
            jax.ShapeDtypeStruct((W, C), F32),
        ),
        in_specs=[vmem] * 7 + [anywhere] * 3,
        out_specs=[anywhere] * 7,
        scratch_shapes=scratch,
        compiler_params=pltpu.CompilerParams(
            collective_id=0, has_side_effects=True, vmem_limit_bytes=60 * 1024 * 1024
        ),
    )(
        ssm_input[0], state_keys[0], state_queries[0], step_raw[0],
        rate_log.reshape(1, NH), skip_gain.reshape(1, NH), norm_gain.reshape(1, C),
        gate_input[0], out_weight, out_grad[0],
    )
    return (
        gi[None], gg[None], gk[None], gq[None], gs[None],
        sm[0:NH, 0], sm[0:NH, 1], sm[NH:24].reshape(C), gw,
    )


def solution(mesh):
    return jax.shard_map(
        body,
        mesh=mesh,
        in_specs=(
            P("dp", "context", "tensor"),
            P("dp", "context", "tensor"),
            P("dp", "context", "tensor"),
            P("dp", "context", "tensor"),
            P("dp", "tensor", "context"),
            P("tensor"),
            P("tensor"),
            P("tensor"),
            P(None, "tensor"),
            P("dp", "context", "tensor"),
        ),
        out_specs=(
            P("dp", "context", "tensor"),
            P("dp", "context", "tensor"),
            P("dp", "context", "tensor"),
            P("dp", "context", "tensor"),
            P("dp", "tensor", "context"),
            P("tensor"),
            P("tensor"),
            P("tensor"),
            P(("dp", "context"), "tensor"),
        ),
        check_vma=False,
    )
```

```python
import jax
import jax.numpy as jnp
from jax import lax
from jax.experimental import pallas as pl
from jax.experimental.pallas import tpu as pltpu
from jax.sharding import PartitionSpec as P

F32 = jnp.float32
BF = jnp.bfloat16
EPSILON = 1e-05
MESH = pl.DeviceIdType.MESH

T = 256
C = 1024
NH = 16
NQ = 8
W = 128
CTX = 16


def dot(a, b):
    return lax.dot_general(a, b, (((1,), (0,)), ((), ())), preferred_element_type=F32)


def dot_t(a, b):
    return lax.dot_general(a, b, (((1,), (1,)), ((), ())), preferred_element_type=F32)


def tdot(a, b):
    return lax.dot_general(a, b, (((0,), (0,)), ((), ())), preferred_element_type=F32)


def split2(v):
    hi = v.astype(BF)
    return hi, (v - hi.astype(F32)).astype(BF)


def split3(v):
    hi = v.astype(BF)
    rest = v - hi.astype(F32)
    mid = rest.astype(BF)
    return hi, mid, (rest - mid.astype(F32)).astype(BF)


def dot3(v, ones):
    parts = dot(jnp.concatenate(split3(v), axis=0), ones)
    return parts[0:NH] + parts[NH : 2 * NH] + parts[2 * NH : 3 * NH]


def iota(shape, axis):
    return lax.broadcasted_iota(jnp.int32, shape, axis)


def lanes(q):
    return pl.ds(pl.multiple_of(q * W, W), W)


def per_head(row):
    own = (iota((NH, C), 1) // 64) == iota((NH, C), 0)
    return jnp.sum(jnp.where(own, row, 0.0), axis=1, keepdims=True)


def kernel(
    x_ref, k_ref, q_ref, step_ref, rate_ref, skip_ref, gain_ref, gate_hbm, w_hbm, og_hbm,
    gi_hbm, gg_hbm, gk_hbm, gq_hbm, gs_hbm, sm_hbm, gw_hbm,
    gate_v, w_v, ogf, ogp, ogt, nm2,
    cumx, eexp, wexp, cum_s, stp_s, kt, qt, k2, q2, sc,
    snd, rcv, ent_s, ent, bsnd, brcv, out_s, outb,
    mt, phi, plo, y_s, gn_s, ga_s, g_s, acc, acc2, invb, mub,
    ds_s, dxw, dq_s, dk_s, rows, accr, accc, accv,
    gi_v, gg_v, gs_v, sm_own, sm_rcv, sm_sum, sm_p,
    sa, sb, owna, ownb, ra, rb, s2a, s2b, r2a, r2b, gw_v,
    in_sem, out_sem, og_ss, og_rs, fa_ss, fa_rs, fb_ss, fb_rs, ba_ss, ba_rs, bb_ss, bb_rs,
    p_ss, p_rs, r1_ss, r1_rs, r2_ss, r2_rs, m_ss, m_rs,
):
    me = lax.axis_index("context")
    myt = lax.axis_index("tensor")
    mydp = lax.axis_index("dp")
    mz, mx = me // 4, me % 4
    other = 1 - mydp
    right, left = (myt + 1) % 4, (myt + 3) % 4

    barrier = pltpu.get_barrier_semaphore()

    def greet(off, carry):
        pl.semaphore_signal(
            barrier, inc=1, device_id={"context": (me + off) % CTX}, device_id_type=MESH
        )
        return carry

    lax.fori_loop(1, CTX, greet, 0)
    pl.semaphore_signal(barrier, inc=1, device_id={"tensor": right}, device_id_type=MESH)
    pl.semaphore_signal(barrier, inc=1, device_id={"tensor": left}, device_id_type=MESH)
    pl.semaphore_signal(barrier, inc=1, device_id={"dp": other}, device_id_type=MESH)

    in_og = pltpu.make_async_copy(og_hbm, ogf.at[myt], in_sem.at[0])
    in_gate = pltpu.make_async_copy(gate_hbm, gate_v, in_sem.at[1])
    in_w = pltpu.make_async_copy(w_hbm, w_v, in_sem.at[2])
    in_og.start()
    in_gate.start()
    in_w.start()

    raw = step_ref[...]
    eye = iota((NH, NH), 0) == iota((NH, NH), 1)
    slope = jnp.sum(jnp.where(eye, jnp.exp(rate_ref[...]), 0.0), axis=1, keepdims=True)
    step = jnp.maximum(raw, 0.0) + jnp.log(1.0 + jnp.exp(-jnp.abs(raw)))
    decay = -slope * step
    upper = (iota((T, T), 0) <= iota((T, T), 1)).astype(BF)
    cum = dot3(decay, upper)
    total = cum[:, T - 1 : T]
    stp_s[...] = step
    cum_s[...] = cum
    spread = ((iota((3 * NH, C), 0) % NH) == (iota((3 * NH, C), 1) // 64)).astype(BF)

    def expand(v, to):
        pieces = jnp.concatenate(split3(v), axis=0).astype(F32)
        turned = jnp.concatenate([pieces, jnp.zeros((W - 3 * NH, T), F32)], axis=0).T
        to[...] = dot(turned[:, : 3 * NH].astype(BF), spread)

    expand(jnp.exp(cum), eexp)
    expand(jnp.exp(total - cum) * step, wexp)
    expand(cum, cumx)
    own = (iota((NH, C), 1) // 64) == iota((NH, C), 0)
    skip_col = jnp.sum(jnp.where(eye, skip_ref[...], 0.0), axis=1, keepdims=True)
    rows[3] = jnp.sum(jnp.where(own, skip_col, 0.0), axis=0, keepdims=True)

    for g in range(2):
        kg = k_ref[:, g * W : (g + 1) * W]
        qg = q_ref[:, g * W : (g + 1) * W]
        kt[g] = kg.T
        qt[g] = qg.T
        k2[g] = jnp.concatenate([kg, kg], axis=1)
        q2[g] = jnp.concatenate([qg, qg], axis=1)

    def local_state(q, carry):
        hi, lo = split2(x_ref[:, lanes(q)].astype(F32) * wexp[:, lanes(q)])
        both = dot(kt[q // 4], jnp.concatenate([hi, lo], axis=1))
        state = both[:, :W] + both[:, W:]
        factor = jnp.broadcast_to(eexp[T - 1 : T, lanes(q)], (8, W))
        snd[2 * q, 0:64] = state[0:64]
        snd[2 * q + 1, 0:64] = state[64:]
        snd[2 * q, 64:72] = factor
        snd[2 * q + 1, 64:72] = factor
        return carry

    lax.fori_loop(0, NQ, local_state, 0)

    pl.semaphore_wait(barrier, CTX + 2)

    def ctx_copy(src, dst, ss, rs, peer, src_slot, dst_slot):
        return pltpu.make_async_remote_copy(
            src_ref=src.at[src_slot],
            dst_ref=dst.at[dst_slot],
            send_sem=ss.at[src_slot],
            recv_sem=rs.at[dst_slot],
            device_id={"context": peer},
            device_id_type=MESH,
        )

    def send_all(src, dst, ss, rs):
        def one(off, carry):
            peer = (me + off) % CTX
            ctx_copy(src, dst, ss, rs, peer, peer, me).start()
            return carry

        lax.fori_loop(1, CTX, one, 0)

    def recv_all(src, dst, ss, rs):
        def one(off, carry):
            peer = (me + off) % CTX
            ctx_copy(src, dst, ss, rs, peer, peer, peer).wait_recv()
            return carry

        lax.fori_loop(1, CTX, one, 0)

    def drain_all(src, dst, ss, rs):
        def one(off, carry):
            peer = (me + off) % CTX
            ctx_copy(src, dst, ss, rs, peer, peer, me).wait_send()
            return carry

        lax.fori_loop(1, CTX, one, 0)

    send_all(snd, rcv, fa_ss, fa_rs)

    def ring(src, dst, sem, peer):
        return pltpu.make_async_remote_copy(
            src_ref=src,
            dst_ref=dst,
            send_sem=og_ss.at[sem],
            recv_sem=og_rs.at[sem],
            device_id={"tensor": peer},
            device_id_type=MESH,
        )

    to_right = ring(og_hbm, ogf.at[myt], 0, right)
    to_left = ring(og_hbm, ogf.at[myt], 1, left)
    to_right.start()
    to_left.start()

    for g in range(2):
        sc[g] = dot_t(q_ref[:, g * W : (g + 1) * W], k_ref[:, g * W : (g + 1) * W])
    causal = iota((T, T), 0) >= iota((T, T), 1)
    first = iota((T, W), 1) < 64

    def within(q, carry):
        xp = x_ref[:, lanes(q)]
        spread_tile = cumx[:, lanes(q)]
        outs = []
        for hh in range(2):
            h = 2 * q + hh
            column = spread_tile[:, 64 * hh : 64 * hh + 1]
            gap = column - cum_s[pl.ds(h, 1), :]
            m = jnp.exp(jnp.where(causal, gap, -1e30)) * stp_s[pl.ds(h, 1), :]
            mt[h] = m
            hi, lo = split2(m * sc[q // 4])
            phi[h] = hi
            plo[h] = lo
            outs.append(dot(hi, xp) + dot(lo, xp))
        y_s[:, lanes(q)] = jnp.where(first, outs[0], outs[1])
        return carry

    lax.fori_loop(0, NQ, within, 0)

    rcv[me] = snd[me]
    recv_all(snd, rcv, fa_ss, fa_rs)
    run = jnp.zeros((64, W), F32)
    for s in range(CTX):
        ent_s[s] = run
        run = rcv[s, 64:65, :] * run + rcv[s, 0:64, :]
    send_all(ent_s, ent, fb_ss, fb_rs)
    ent[me] = ent_s[me]

    in_og.wait()
    to_right.wait_recv()
    relay_right = ring(ogf.at[left, 0:128], ogf.at[left, 0:128], 2, right)
    relay_right.start()
    to_left.wait_recv()
    relay_left = ring(ogf.at[right, 128:256], ogf.at[right, 128:256], 3, left)
    relay_left.start()
    in_w.wait()

    def project(chunk, first_term):
        def one(n, carry):
            part = dot(
                ogf[chunk], w_v[pl.ds(pl.multiple_of(chunk * C, C), C), pl.ds(pl.multiple_of(n * 256, 256), 256)]
            )
            where = pl.ds(pl.multiple_of(n * 256, 256), 256)
            gn_s[:, where] = part if first_term else gn_s[:, where] + part
            return carry

        lax.fori_loop(0, 4, one, 0)

    project(myt, True)
    project(left, False)
    project(right, False)
    relay_right.wait_recv()
    relay_left.wait_recv()

    def pair(src, dst, sem):
        return pltpu.make_async_remote_copy(
            src_ref=src,
            dst_ref=dst,
            send_sem=p_ss.at[sem],
            recv_sem=p_rs.at[sem],
            device_id={"dp": other},
            device_id_type=MESH,
        )

    pair_og = [pair(ogf.at[2 * other + i], ogp.at[i], i) for i in range(2)]
    for copy in pair_og:
        copy.start()
    project((myt + 2) % 4, False)

    def turn_own(i, carry):
        at = pl.ds(pl.multiple_of(i * W, W), W)
        ogt[at, 0:T] = ogf[2 * mydp + i // 8, :, lanes(i % 8)].T
        return carry

    lax.fori_loop(0, 16, turn_own, 0)
    for copy in pair_og:
        copy.wait_recv()

    def turn_pair(i, carry):
        at = pl.ds(pl.multiple_of(i * W, W), W)
        ogt[at, T : 2 * T] = ogp[i // 8, :, lanes(i % 8)].T
        return carry

    lax.fori_loop(0, 16, turn_pair, 0)
    in_gate.wait()
    recv_all(ent_s, ent, fb_ss, fb_rs)

    acc[...] = jnp.zeros_like(acc)
    acc2[...] = jnp.zeros_like(acc2)

    def entering(q):
        return jnp.concatenate([ent[2 * q], ent[2 * q + 1]], axis=0)

    def scan_out(q, carry):
        g = q // 4
        carried = dot(q2[g], jnp.concatenate(split2(entering(q)), axis=0))
        y = y_s[:, lanes(q)] + eexp[:, lanes(q)] * carried
        y_s[:, lanes(q)] = y
        ssd = y + rows[3, :, lanes(q)] * x_ref[:, lanes(q)].astype(F32)
        gate = gate_v[:, lanes(q)].astype(F32)
        gated = ssd * (gate / (1.0 + jnp.exp(-gate)))
        ga_s[:, lanes(q)] = gated
        acc[g] += gated * gated
        acc2[g] += gn_s[:, lanes(q)] * gain_ref[:, lanes(q)] * gated
        return carry

    lax.fori_loop(0, NQ, scan_out, 0)
    for g in range(2):
        mean = jnp.sum(acc[g], axis=1, keepdims=True) * (1.0 / 512)
        inverse = lax.rsqrt(mean + EPSILON)
        shift = jnp.sum(acc2[g], axis=1, keepdims=True) * (1.0 / 512)
        invb[g] = jnp.broadcast_to(inverse, (T, W))
        mub[g] = jnp.broadcast_to(shift * inverse * inverse, (T, W))

    def normalize(q, carry):
        value = ga_s[:, lanes(q)] * invb[q // 4] * gain_ref[:, lanes(q)]
        nm2[0:T, lanes(q)] = value.astype(BF)
        return carry

    lax.fori_loop(0, NQ, normalize, 0)
    pair_nm = pair(nm2.at[0:T], nm2.at[T : 2 * T], 2)
    pair_nm.start()

    def norm_back(q, carry):
        g = q // 4
        gated = ga_s[:, lanes(q)]
        inverse = invb[g]
        gn = gn_s[:, lanes(q)]
        d_gated = inverse * (gn * gain_ref[:, lanes(q)] - gated * mub[g])
        rows[0, :, lanes(q)] = jnp.sum(gn * gated * inverse, axis=0, keepdims=True)
        gate = gate_v[:, lanes(q)].astype(F32)
        xv = x_ref[:, lanes(q)].astype(F32)
        sig = 1.0 / (1.0 + jnp.exp(-gate))
        silu = gate * sig
        y = y_s[:, lanes(q)]
        ssd = y + rows[3, :, lanes(q)] * xv
        gg_v[:, lanes(q)] = (d_gated * ssd * (sig * (1.0 + gate - silu))).astype(BF)
        grad = d_gated * silu
        g_s[:, lanes(q)] = grad
        rows[1, :, lanes(q)] = jnp.sum(grad * xv, axis=0, keepdims=True)
        hi, lo = split2(eexp[:, lanes(q)] * grad)
        both = dot(qt[g], jnp.concatenate([hi, lo], axis=1))
        into = both[:, :W] + both[:, W:]
        bsnd[2 * q] = into[0:64]
        bsnd[2 * q + 1] = into[64:]
        return carry

    lax.fori_loop(0, NQ, norm_back, 0)
    out_gg = pltpu.make_async_copy(gg_v, gg_hbm, out_sem.at[0])
    out_gg.start()
    send_all(bsnd, brcv, ba_ss, ba_rs)

    pair_nm.wait_recv()

    def weight_block(block, half):
        at = pl.ds(pl.multiple_of(block * W, W), W)
        return dot(ogt[at, :], nm2[:, half * 512 : half * 512 + 512])

    def phase1(src, dst, sem, peer):
        return pltpu.make_async_remote_copy(
            src_ref=src,
            dst_ref=dst,
            send_sem=r1_ss.at[sem],
            recv_sem=r1_rs.at[sem],
            device_id={"context": peer},
            device_id_type=MESH,
        )

    def phase2(src, dst, sem, peer):
        return pltpu.make_async_remote_copy(
            src_ref=src,
            dst_ref=dst,
            send_sem=r2_ss.at[sem],
            recv_sem=r2_rs.at[sem],
            device_id={"context": peer},
            device_id_type=MESH,
        )

    sends1 = []
    for d in (2, 1, 3):
        px = (mx + d) % 4
        pz = (mz + d) % 4

        def fill_a(i, carry, px=px, d=d):
            sa[d - 1, i] = weight_block(i * 4 + px, 0).astype(BF)
            return carry

        lax.fori_loop(0, 4, fill_a, 0)
        copy = phase1(sa.at[d - 1], ra.at[d - 1], d - 1, mz * 4 + px)
        copy.start()
        sends1.append(copy)

        def fill_b(i, carry, pz=pz, d=d):
            sb[d - 1, i] = weight_block(pz * 4 + i, 1).astype(BF)
            return carry

        lax.fori_loop(0, 4, fill_b, 0)
        copy = phase1(sb.at[d - 1], rb.at[d - 1], 3 + d - 1, pz * 4 + mx)
        copy.start()
        sends1.append(copy)

    def fill_own(i, carry):
        owna[i] = weight_block(i * 4 + mx, 0)
        ownb[i] = weight_block(mz * 4 + i, 1)
        return carry

    lax.fori_loop(0, 4, fill_own, 0)

    brcv[me] = bsnd[me]
    recv_all(bsnd, brcv, ba_ss, ba_rs)
    run = jnp.zeros((64, W), F32)
    for s in range(CTX - 1, -1, -1):
        out_s[s] = run
        run = brcv[s] + rcv[s, 64:65, :] * run
    send_all(out_s, outb, bb_ss, bb_rs)
    outb[me] = out_s[me]

    ds_s[...] = jnp.zeros_like(ds_s)
    dq_s[...] = jnp.zeros_like(dq_s)
    dk_s[...] = jnp.zeros_like(dk_s)
    accr[...] = jnp.zeros_like(accr)
    accc[...] = jnp.zeros_like(accc)
    accv[...] = jnp.zeros_like(accv)

    def head_sums(q, value):
        row, lane = iota((NH, 2 * W), 0), iota((NH, 2 * W), 1) % W
        pick = (row == 2 * q + lane // 64).astype(BF)
        return dot_t(pick, jnp.concatenate(split2(value), axis=1))

    def within_back(q, carry):
        g = q // 4
        xp = x_ref[:, lanes(q)]
        grad = g_s[:, lanes(q)]
        ghi, glo = split2(grad)
        gthi, gtlo = ghi.T, glo.T
        x2 = jnp.concatenate([xp, xp], axis=1)
        zero = jnp.zeros((T, W), BF)
        parts = []
        total_ds = ds_s[g]
        for hh in range(2):
            h = 2 * q + hh
            keep = first if hh == 0 else jnp.logical_not(first)
            g2 = jnp.concatenate([jnp.where(keep, ghi, zero), jnp.where(keep, glo, zero)], axis=1)
            total_ds = total_ds + dot_t(g2, x2) * mt[h]
            a, b = gthi[64 * hh : 64 * hh + 64], gtlo[64 * hh : 64 * hh + 64]
            both = dot(jnp.concatenate([a, b], axis=0), phi[h])
            parts.append(both[0:64] + both[64:] + dot(a, plo[h]))
        ds_s[g] = total_ds
        dxw[:, lanes(q)] = jnp.concatenate(parts, axis=0).T
        accr[...] += head_sums(q, grad * y_s[:, lanes(q)])
        ehi, elo = split2(eexp[:, lanes(q)] * grad)
        shi, slo = split2(entering(q))
        to_q = dot_t(jnp.concatenate([ehi, elo], axis=1), jnp.concatenate([shi, shi], axis=1))
        dq_s[:, lanes(g)] += to_q + dot_t(ehi, slo)
        return carry

    lax.fori_loop(0, NQ, within_back, 0)
    for g in range(2):
        hi, lo = split2(ds_s[g])
        kg = k_ref[:, g * W : (g + 1) * W]
        qg = q_ref[:, g * W : (g + 1) * W]
        dq_s[:, g * W : (g + 1) * W] += dot(hi, kg) + dot(lo, kg)
        dk_s[:, g * W : (g + 1) * W] = tdot(hi, qg) + tdot(lo, qg)
    out_gq = pltpu.make_async_copy(dq_s, gq_hbm, out_sem.at[1])
    out_gq.start()

    recv_all(out_s, outb, bb_ss, bb_rs)

    def state_back(q, carry):
        g = q // 4
        d_state = jnp.concatenate([outb[2 * q], outb[2 * q + 1]], axis=0)
        dhi, dlo = split2(d_state)
        rows[2, :, lanes(q)] = jnp.sum(d_state * entering(q), axis=0, keepdims=True)
        weight = wexp[:, lanes(q)]
        xv = x_ref[:, lanes(q)].astype(F32)
        via = weight * dot(k2[g], jnp.concatenate([dhi, dlo], axis=0))
        dx = dxw[:, lanes(q)] + via
        gi_v[:, lanes(q)] = (dx + rows[3, :, lanes(q)] * g_s[:, lanes(q)]).astype(BF)
        accc[...] += head_sums(q, xv * dx)
        accv[...] += head_sums(q, xv * via)
        whi, wlo = split2(weight * xv)
        to_k = dot_t(jnp.concatenate([whi, wlo], axis=1), jnp.concatenate([dhi, dhi], axis=1))
        dk_s[:, lanes(g)] += to_k + dot_t(whi, dlo)
        return carry

    lax.fori_loop(0, NQ, state_back, 0)
    out_gi = pltpu.make_async_copy(gi_v, gi_hbm, out_sem.at[2])
    out_gi.start()
    out_gk = pltpu.make_async_copy(dk_s, gk_hbm, out_sem.at[3])
    out_gk.start()

    raw = step_ref[...]
    slope = jnp.sum(jnp.where(eye, jnp.exp(rate_ref[...]), 0.0), axis=1, keepdims=True)
    step = stp_s[...]
    lower = (iota((T, T), 0) >= iota((T, T), 1)).astype(BF)
    after = dot3(accr[...] - accc[...], lower)
    log_grad = per_head(rows[2] * eexp[T - 1 : T, :])
    d_total = jnp.sum(accv[...], axis=1, keepdims=True) + log_grad
    d_decay = after + d_total
    gs_v[...] = (accc[...] / step - slope * d_decay) / (1.0 + jnp.exp(-raw))
    out_gs = pltpu.make_async_copy(gs_v, gs_hbm, out_sem.at[4])
    out_gs.start()
    rate_part = jnp.sum(d_decay * (-slope * step), axis=1, keepdims=True)
    lane = iota((NH, W), 1)
    sm_own[0:NH] = jnp.where(lane == 0, rate_part, jnp.where(lane == 1, per_head(rows[1]), 0.0))
    for i in range(NQ):
        sm_own[NH + i : NH + i + 1] = rows[0, :, i * W : (i + 1) * W]

    def small_copy(peer, slot):
        return pltpu.make_async_remote_copy(
            src_ref=sm_own,
            dst_ref=sm_rcv.at[slot],
            send_sem=m_ss.at[peer],
            recv_sem=m_rs.at[slot],
            device_id={"context": peer},
            device_id_type=MESH,
        )

    def small_send(off, carry):
        small_copy((me + off) % CTX, me).start()
        return carry

    def small_recv(off, carry):
        small_copy((me + off) % CTX, (me + off) % CTX).wait_recv()
        return carry

    def small_drain(off, carry):
        small_copy((me + off) % CTX, me).wait_send()
        return carry

    lax.fori_loop(1, CTX, small_send, 0)
    sm_rcv[me] = sm_own[...]

    for d in (1, 3, 2):
        phase1(sa.at[d - 1], ra.at[d - 1], d - 1, mz * 4 + mx).wait_recv()
        phase1(sb.at[d - 1], rb.at[d - 1], 3 + d - 1, mz * 4 + mx).wait_recv()

    def sum_a(i):
        value = owna[i]
        for d in range(3):
            value = value + ra[d, i].astype(F32)
        return value

    def sum_b(i):
        value = ownb[i]
        for d in range(3):
            value = value + rb[d, i].astype(F32)
        return value

    sends2 = []
    for d in (2, 1, 3):
        pz = (mz + d) % 4
        px = (mx + d) % 4
        s2a[d - 1] = sum_a(pz).astype(BF)
        copy = phase2(s2a.at[d - 1], r2a.at[d - 1], d - 1, pz * 4 + mx)
        copy.start()
        sends2.append(copy)
        s2b[d - 1] = sum_b(px).astype(BF)
        copy = phase2(s2b.at[d - 1], r2b.at[d - 1], 3 + d - 1, mz * 4 + px)
        copy.start()
        sends2.append(copy)
    gw_v[:, 0:512] = sum_a(mz)
    gw_v[:, 512:1024] = sum_b(mx)

    lax.fori_loop(1, CTX, small_recv, 0)
    value = sm_rcv[0]
    for s in range(1, CTX):
        value = value + sm_rcv[s]
    sm_sum[...] = value
    pair_sm = pair(sm_sum, sm_p, 3)
    pair_sm.start()

    for copy in sends2:
        copy.wait_recv()
    for d in range(3):
        gw_v[:, 0:512] += r2a[d].astype(F32)
        gw_v[:, 512:1024] += r2b[d].astype(F32)
    out_gw = pltpu.make_async_copy(gw_v, gw_hbm, out_sem.at[5])
    out_gw.start()

    pair_sm.wait()
    sm_sum[...] += sm_p[...]
    out_sm = pltpu.make_async_copy(sm_sum, sm_hbm, out_sem.at[6])
    out_sm.start()

    drain_all(snd, rcv, fa_ss, fa_rs)
    drain_all(ent_s, ent, fb_ss, fb_rs)
    drain_all(bsnd, brcv, ba_ss, ba_rs)
    drain_all(out_s, outb, bb_ss, bb_rs)
    lax.fori_loop(1, CTX, small_drain, 0)
    for copy in (to_right, to_left, relay_right, relay_left, *pair_og, pair_nm, *sends1, *sends2):
        copy.wait_send()
    for copy in (out_gg, out_gq, out_gi, out_gk, out_gs, out_gw, out_sm):
        copy.wait()


def hand_out(
    gi_in, gg_in, gk_in, gq_in, gs_in, sm_in, gw_in,
    gi_out, gg_out, gk_out, gq_out, gs_out, gw_out, rate_ref, skip_ref, norm_ref,
    gi_v, gg_v, gk_v, gq_v, gs_v, gw_v, sm_v, in_sem, out_sem,
):
    small = pltpu.make_async_copy(sm_in, sm_v, in_sem.at[6])
    small.start()
    ways = (
        (gi_in, gi_v, gi_out), (gg_in, gg_v, gg_out), (gw_in, gw_v, gw_out),
        (gk_in, gk_v, gk_out), (gq_in, gq_v, gq_out), (gs_in, gs_v, gs_out),
    )
    into = [pltpu.make_async_copy(w[0], w[1], in_sem.at[i]) for i, w in enumerate(ways)]
    out = [pltpu.make_async_copy(w[1], w[2], out_sem.at[i]) for i, w in enumerate(ways)]
    for copy in into:
        copy.start()
    small.wait()
    eye = iota((NH, W), 0) == iota((NH, W), 1)
    for lane, ref in ((0, rate_ref), (1, skip_ref)):
        column = sm_v[0:NH, lane : lane + 1]
        ref[...] = jnp.sum(jnp.where(eye, column, 0.0), axis=0, keepdims=True)[:, 0:NH]
    for i in range(NQ):
        norm_ref[:, i * W : (i + 1) * W] = sm_v[NH + i : NH + i + 1]
    for before, after in zip(into, out):
        before.wait()
        after.start()
    for copy in out:
        copy.wait()


def body(
    ssm_input, gate_input, state_keys, state_queries, step_raw,
    rate_log, skip_gain, norm_gain, out_weight, out_grad,
):
    vmem, anywhere = pl.BlockSpec(memory_space=pltpu.VMEM), pl.BlockSpec(memory_space=pl.ANY)
    V, S = pltpu.VMEM, pltpu.SemaphoreType.DMA
    scratch = [
        V((T, C), BF), V((4 * C, C), BF), V((4, T, C), BF), V((2, T, C), BF), V((2 * C, 2 * T), BF),
        V((2 * T, C), BF),
        V((T, C), F32), V((T, C), F32), V((T, C), F32), V((NH, T), F32), V((NH, T), F32),
        V((2, W, T), BF), V((2, W, T), BF), V((2, T, 2 * W), BF), V((2, T, 2 * W), BF),
        V((2, T, T), F32),
        V((CTX, 72, W), F32), V((CTX, 72, W), F32), V((CTX, 64, W), F32), V((CTX, 64, W), F32),
        V((CTX, 64, W), F32), V((CTX, 64, W), F32), V((CTX, 64, W), F32), V((CTX, 64, W), F32),
        V((NH, T, T), F32), V((NH, T, T), BF), V((NH, T, T), BF),
        V((T, C), F32), V((T, C), F32), V((T, C), F32), V((T, C), F32),
        V((2, T, W), F32), V((2, T, W), F32), V((2, T, W), F32), V((2, T, W), F32),
        V((2, T, T), F32), V((T, C), F32), V((T, 2 * W), F32), V((T, 2 * W), F32),
        V((4, 1, C), F32), V((NH, T), F32), V((NH, T), F32), V((NH, T), F32),
        V((T, C), BF), V((T, C), BF), V((NH, T), F32),
        V((24, W), F32), V((CTX, 24, W), F32), V((24, W), F32), V((24, W), F32),
        V((3, 4, W, 512), BF), V((3, 4, W, 512), BF), V((4, W, 512), F32), V((4, W, 512), F32),
        V((3, 4, W, 512), BF), V((3, 4, W, 512), BF),
        V((3, W, 512), BF), V((3, W, 512), BF), V((3, W, 512), BF), V((3, W, 512), BF),
        V((W, C), F32),
        S((3,)), S((7,)), S((4,)), S((4,)),
        S((CTX,)), S((CTX,)), S((CTX,)), S((CTX,)), S((CTX,)), S((CTX,)), S((CTX,)), S((CTX,)),
        S((4,)), S((4,)), S((6,)), S((6,)), S((6,)), S((6,)), S((CTX,)), S((CTX,)),
    ]
    parts = pl.pallas_call(
        kernel,
        out_shape=(
            jax.ShapeDtypeStruct((T, C), BF),
            jax.ShapeDtypeStruct((T, C), BF),
            jax.ShapeDtypeStruct((T, 2 * W), F32),
            jax.ShapeDtypeStruct((T, 2 * W), F32),
            jax.ShapeDtypeStruct((NH, T), F32),
            jax.ShapeDtypeStruct((24, W), F32),
            jax.ShapeDtypeStruct((W, C), F32),
        ),
        in_specs=[vmem] * 7 + [anywhere] * 3,
        out_specs=[anywhere] * 7,
        scratch_shapes=scratch,
        compiler_params=pltpu.CompilerParams(
            collective_id=0, has_side_effects=True, vmem_limit_bytes=60 * 1024 * 1024
        ),
    )(
        ssm_input[0], state_keys[0], state_queries[0], step_raw[0],
        rate_log.reshape(1, NH), skip_gain.reshape(1, NH), norm_gain.reshape(1, C),
        gate_input[0], out_weight, out_grad[0],
    )
    gi, gg, gk, gq, gs, gw, rate, skip, norm = pl.pallas_call(
        hand_out,
        out_shape=(
            jax.ShapeDtypeStruct((T, C), BF),
            jax.ShapeDtypeStruct((T, C), BF),
            jax.ShapeDtypeStruct((T, 2 * W), F32),
            jax.ShapeDtypeStruct((T, 2 * W), F32),
            jax.ShapeDtypeStruct((NH, T), F32),
            jax.ShapeDtypeStruct((W, C), F32),
            jax.ShapeDtypeStruct((1, NH), F32),
            jax.ShapeDtypeStruct((1, NH), F32),
            jax.ShapeDtypeStruct((1, C), F32),
        ),
        in_specs=[anywhere] * 7,
        out_specs=[anywhere] * 6 + [vmem] * 3,
        scratch_shapes=[
            V((T, C), BF), V((T, C), BF), V((T, 2 * W), F32), V((T, 2 * W), F32), V((NH, T), F32),
            V((W, C), F32), V((24, W), F32), S((7,)), S((6,)),
        ],
    )(*parts)
    return (
        gi[None], gg[None], gk[None], gq[None], gs[None],
        rate.reshape(NH), skip.reshape(NH), norm.reshape(C), gw,
    )


def solution(mesh):
    return jax.shard_map(
        body,
        mesh=mesh,
        in_specs=(
            P("dp", "context", "tensor"),
            P("dp", "context", "tensor"),
            P("dp", "context", "tensor"),
            P("dp", "context", "tensor"),
            P("dp", "tensor", "context"),
            P("tensor"),
            P("tensor"),
            P("tensor"),
            P(None, "tensor"),
            P("dp", "context", "tensor"),
        ),
        out_specs=(
            P("dp", "context", "tensor"),
            P("dp", "context", "tensor"),
            P("dp", "context", "tensor"),
            P("dp", "context", "tensor"),
            P("dp", "tensor", "context"),
            P("tensor"),
            P("tensor"),
            P("tensor"),
            P(("dp", "context"), "tensor"),
        ),
        check_vma=False,
    )
```

```python
import jax
import jax.numpy as jnp
from jax import lax
from jax.experimental import pallas as pl
from jax.experimental.pallas import tpu as pltpu
from jax.sharding import PartitionSpec as P

F32 = jnp.float32
BF = jnp.bfloat16
EPSILON = 1e-05
MESH = pl.DeviceIdType.MESH

T = 256
C = 1024
NH = 16
NQ = 8
W = 128
CTX = 16


def dot(a, b):
    return lax.dot_general(a, b, (((1,), (0,)), ((), ())), preferred_element_type=F32)


def dot_t(a, b):
    return lax.dot_general(a, b, (((1,), (1,)), ((), ())), preferred_element_type=F32)


def tdot(a, b):
    return lax.dot_general(a, b, (((0,), (0,)), ((), ())), preferred_element_type=F32)


def split2(v):
    hi = v.astype(BF)
    return hi, (v - hi.astype(F32)).astype(BF)


def split3(v):
    hi = v.astype(BF)
    rest = v - hi.astype(F32)
    mid = rest.astype(BF)
    return hi, mid, (rest - mid.astype(F32)).astype(BF)


def dot3(v, ones):
    parts = dot(jnp.concatenate(split3(v), axis=0), ones)
    return parts[0:NH] + parts[NH : 2 * NH] + parts[2 * NH : 3 * NH]


def iota(shape, axis):
    return lax.broadcasted_iota(jnp.int32, shape, axis)


def lanes(q):
    return pl.ds(pl.multiple_of(q * W, W), W)


def per_head(row):
    own = (iota((NH, C), 1) // 64) == iota((NH, C), 0)
    return jnp.sum(jnp.where(own, row, 0.0), axis=1, keepdims=True)


def kernel(
    x_hbm, k_hbm, q_hbm, step_hbm, rate_hbm, skip_hbm, gain_hbm, gate_hbm, w_hbm, og_hbm,
    gi_v, gg_v, dk_s, dq_s, gs_v, gw_v, ea_own, la_own,
    x_ref, k_ref, q_ref, step_ref, rate_ref, skip_ref, gain_ref,
    gate_v, w_v, ogf, ogp, ogt, nm2,
    cumx, eexp, wexp, cum_s, stp_s, kt, qt, sc,
    snd, rcv, ent_s, ent, bsnd, brcv, out_s, outb,
    silu_s, bend_s, skx_s, mt, phi, plo, y_s, gn_s, ga_s, g_s, acc, acc2, invb, mub,
    ds_s, dxw, rows, accr, accc, accv,
    ea_rcv, ea_p, la_rcv, la_p, s1, r1, own1, s2, r2, fwd2,
    in_sem, og_ss, og_rs, fa_ss, fa_rs, fb_ss, fb_rs, ba_ss, ba_rs, bb_ss, bb_rs,
    p_ss, p_rs, r1_ss, r1_rs, r2_ss, r2_rs, ea_ss, ea_rs, la_ss, la_rs,
):
    me = lax.axis_index("context")
    myt = lax.axis_index("tensor")
    mydp = lax.axis_index("dp")
    mz, mx = me // 4, me % 4
    other = 1 - mydp
    right, left = (myt + 1) % 4, (myt + 3) % 4

    barrier = pltpu.get_barrier_semaphore()

    def greet(off, carry):
        pl.semaphore_signal(
            barrier, inc=1, device_id={"context": (me + off) % CTX}, device_id_type=MESH
        )
        return carry

    pl.semaphore_signal(barrier, inc=1, device_id={"tensor": right}, device_id_type=MESH)
    pl.semaphore_signal(barrier, inc=1, device_id={"tensor": left}, device_id_type=MESH)
    lax.fori_loop(1, CTX, greet, 0)
    pl.semaphore_signal(barrier, inc=1, device_id={"dp": other}, device_id_type=MESH)

    loads = [
        pltpu.make_async_copy(src, dst, in_sem.at[i])
        for i, (src, dst) in enumerate(
            (
                (step_hbm, step_ref), (rate_hbm, rate_ref), (skip_hbm, skip_ref), (k_hbm, k_ref),
                (x_hbm, x_ref), (q_hbm, q_ref), (gain_hbm, gain_ref), (og_hbm, ogf.at[myt]),
                (gate_hbm, gate_v), (w_hbm, w_v),
            )
        )
    ]
    for copy in loads:
        copy.start()
    for copy in loads[:3]:
        copy.wait()

    raw = step_ref[...]
    eye = iota((NH, NH), 0) == iota((NH, NH), 1)
    slope = jnp.sum(jnp.where(eye, jnp.exp(rate_ref[...]), 0.0), axis=1, keepdims=True)
    step = jnp.maximum(raw, 0.0) + jnp.log(1.0 + jnp.exp(-jnp.abs(raw)))
    decay = -slope * step
    upper = (iota((T, T), 0) <= iota((T, T), 1)).astype(BF)
    cum = dot3(decay, upper)
    total = cum[:, T - 1 : T]
    stp_s[...] = step
    cum_s[...] = cum
    spread = ((iota((3 * NH, C), 0) % NH) == (iota((3 * NH, C), 1) // 64)).astype(BF)

    def expand(v, to):
        pieces = jnp.concatenate(split3(v), axis=0).astype(F32)
        turned = jnp.concatenate([pieces, jnp.zeros((W - 3 * NH, T), F32)], axis=0).T
        to[...] = dot(turned[:, : 3 * NH].astype(BF), spread)

    expand(jnp.exp(total - cum) * step, wexp)
    expand(jnp.exp(cum), eexp)
    own = (iota((NH, C), 1) // 64) == iota((NH, C), 0)
    skip_col = jnp.sum(jnp.where(eye, skip_ref[...], 0.0), axis=1, keepdims=True)
    rows[3] = jnp.sum(jnp.where(own, skip_col, 0.0), axis=0, keepdims=True)

    loads[3].wait()
    for g in range(2):
        kt[g] = k_ref[:, g * W : (g + 1) * W].T
    loads[4].wait()

    def local_state(q, carry):
        hi, lo = split2(x_ref[:, lanes(q)].astype(F32) * wexp[:, lanes(q)])
        both = dot(kt[q // 4], jnp.concatenate([hi, lo], axis=1))
        state = both[:, :W] + both[:, W:]
        factor = jnp.broadcast_to(eexp[T - 1 : T, lanes(q)], (8, W))
        snd[2 * q, 0:64] = state[0:64]
        snd[2 * q + 1, 0:64] = state[64:]
        snd[2 * q, 64:72] = factor
        snd[2 * q + 1, 64:72] = factor
        return carry

    lax.fori_loop(0, NQ, local_state, 0)

    pl.semaphore_wait(barrier, CTX + 2)

    def ctx_copy(src, dst, ss, rs, peer, src_slot, dst_slot):
        return pltpu.make_async_remote_copy(
            src_ref=src.at[src_slot],
            dst_ref=dst.at[dst_slot],
            send_sem=ss.at[src_slot],
            recv_sem=rs.at[dst_slot],
            device_id={"context": peer},
            device_id_type=MESH,
        )

    def send_all(src, dst, ss, rs):
        def one(off, carry):
            peer = (me + off) % CTX
            ctx_copy(src, dst, ss, rs, peer, peer, me).start()
            return carry

        lax.fori_loop(1, CTX, one, 0)

    def recv_all(src, dst, ss, rs):
        def one(off, carry):
            peer = (me + off) % CTX
            ctx_copy(src, dst, ss, rs, peer, peer, peer).wait_recv()
            return carry

        lax.fori_loop(1, CTX, one, 0)

    def drain_all(src, dst, ss, rs):
        def one(off, carry):
            peer = (me + off) % CTX
            ctx_copy(src, dst, ss, rs, peer, peer, me).wait_send()
            return carry

        lax.fori_loop(1, CTX, one, 0)

    def ring(src, dst, sem, peer):
        return pltpu.make_async_remote_copy(
            src_ref=src,
            dst_ref=dst,
            send_sem=og_ss.at[sem],
            recv_sem=og_rs.at[sem],
            device_id={"tensor": peer},
            device_id_type=MESH,
        )

    top, low = pl.ds(0, 128), pl.ds(128, 128)
    to_right = [ring(og_hbm.at[h], ogf.at[myt, h], i, right) for i, h in enumerate((top, low))]
    to_left = [ring(og_hbm.at[h], ogf.at[myt, h], 2 + i, left) for i, h in enumerate((low, top))]
    to_right[0].start()
    to_left[0].start()
    send_all(snd, rcv, fa_ss, fa_rs)

    to_right[1].start()
    to_left[1].start()

    expand(cum_s[...], cumx)
    loads[5].wait()
    for g in range(2):
        qg = q_ref[:, g * W : (g + 1) * W]
        qt[g] = qg.T
        sc[g] = dot_t(qg, k_ref[:, g * W : (g + 1) * W])
    causal = iota((T, T), 0) >= iota((T, T), 1)
    first = iota((T, W), 1) < 64

    def within(q, carry):
        xp = x_ref[:, lanes(q)]
        spread_tile = cumx[:, lanes(q)]
        outs = []
        for hh in range(2):
            h = 2 * q + hh
            column = spread_tile[:, 64 * hh : 64 * hh + 1]
            gap = column - cum_s[pl.ds(h, 1), :]
            m = jnp.exp(jnp.where(causal, gap, -1e30)) * stp_s[pl.ds(h, 1), :]
            mt[h] = m
            hi, lo = split2(m * sc[q // 4])
            phi[h] = hi
            plo[h] = lo
            outs.append(dot(hi, xp) + dot(lo, xp))
        y_s[:, lanes(q)] = jnp.where(first, outs[0], outs[1])
        return carry

    lax.fori_loop(0, NQ, within, 0)

    to_right[0].wait_recv()
    relay_right = ring(ogf.at[left, top], ogf.at[left, top], 4, right)
    relay_right.start()
    to_left[0].wait_recv()
    relay_left = ring(ogf.at[right, low], ogf.at[right, low], 5, left)
    relay_left.start()
    loads[8].wait()

    def gates(q, carry):
        gate = gate_v[:, lanes(q)].astype(F32)
        sig = 1.0 / (1.0 + jnp.exp(-gate))
        silu = gate * sig
        silu_s[:, lanes(q)] = silu
        bend_s[:, lanes(q)] = sig * (1.0 + gate - silu)
        skx_s[:, lanes(q)] = rows[3, :, lanes(q)] * x_ref[:, lanes(q)].astype(F32)
        return carry

    lax.fori_loop(0, NQ, gates, 0)

    rcv[me] = snd[me]
    recv_all(snd, rcv, fa_ss, fa_rs)
    run = jnp.zeros((64, W), F32)
    for s in range(CTX):
        ent_s[s] = run
        run = rcv[s, 64:65] * run + rcv[s, 0:64]
    send_all(ent_s, ent, fb_ss, fb_rs)
    ent[me] = ent_s[me]

    loads[7].wait()
    loads[9].wait()

    def pair(src, dst, sem):
        return pltpu.make_async_remote_copy(
            src_ref=src,
            dst_ref=dst,
            send_sem=p_ss.at[sem],
            recv_sem=p_rs.at[sem],
            device_id={"dp": other},
            device_id_type=MESH,
        )

    def pair_og(chunk):
        return pair(ogf.at[chunk], ogp.at[chunk % 2], chunk % 2)

    def hand_over(chunk):
        @pl.when(chunk // 2 == other)
        def _():
            pair_og(chunk).start()

        @pl.when(chunk // 2 == mydp)
        def _():
            def turn(i, carry):
                at = pl.ds(pl.multiple_of((chunk % 2) * C + i * W, W), W)
                ogt[at, 0:T] = ogf[chunk, :, lanes(i)].T
                return carry

            lax.fori_loop(0, 8, turn, 0)

    def project(chunk, first_term):
        def one(n, carry):
            where = pl.ds(pl.multiple_of(n * 256, 256), 256)
            part = dot(ogf[chunk], w_v[pl.ds(pl.multiple_of(chunk * C, C), C), where])
            gn_s[:, where] = part if first_term else gn_s[:, where] + part
            return carry

        lax.fori_loop(0, 4, one, 0)

    def take(chunk, first_term):
        hand_over(chunk)
        project(chunk, first_term)

    def turn_pair(chunk):
        @pl.when(chunk // 2 == mydp)
        def _():
            pair_og(chunk).wait_recv()

            def turn(i, carry):
                at = pl.ds(pl.multiple_of((chunk % 2) * C + i * W, W), W)
                ogt[at, T : 2 * T] = ogp[chunk % 2, :, lanes(i)].T
                return carry

            lax.fori_loop(0, 8, turn, 0)

    take(myt, True)
    loads[6].wait()
    to_right[1].wait_recv()
    take(left, False)
    turn_pair(myt)
    to_left[1].wait_recv()
    take(right, False)
    turn_pair(left)
    recv_all(ent_s, ent, fb_ss, fb_rs)

    acc[...] = jnp.zeros_like(acc)

    def entering(q):
        return jnp.concatenate([ent[2 * q], ent[2 * q + 1]], axis=0)

    def group_q(q):
        return q_ref[:, lanes(q // 4)]

    def scan_out(q, carry):
        g = q // 4
        twice = jnp.concatenate([group_q(q), group_q(q)], axis=1)
        carried = dot(twice, jnp.concatenate(split2(entering(q)), axis=0))
        y = y_s[:, lanes(q)] + eexp[:, lanes(q)] * carried
        y_s[:, lanes(q)] = y
        gated = (y + skx_s[:, lanes(q)]) * silu_s[:, lanes(q)]
        ga_s[:, lanes(q)] = gated
        acc[g] += gated * gated
        return carry

    lax.fori_loop(0, NQ, scan_out, 0)
    for g in range(2):
        mean = jnp.sum(acc[g], axis=1, keepdims=True) * (1.0 / 512)
        invb[g] = jnp.broadcast_to(lax.rsqrt(mean + EPSILON), (T, W))

    def normalize(q, carry):
        value = ga_s[:, lanes(q)] * invb[q // 4] * gain_ref[:, lanes(q)]
        nm2[0:T, lanes(q)] = value.astype(BF)
        return carry

    lax.fori_loop(0, NQ, normalize, 0)
    pair_nm = pair(nm2.at[0:T], nm2.at[T : 2 * T], 2)
    pair_nm.start()

    relay_right.wait_recv()
    relay_left.wait_recv()
    hand_over((myt + 2) % 4)
    turn_pair(right)
    turn_pair((myt + 2) % 4)
    pair_nm.wait_recv()

    def ahead(v):
        return (v + 1 + 2 * mydp) % 4

    def behind(v):
        return (v + 3 - 2 * mydp) % 4

    def far(v):
        return (v + 2) % 4

    def along(phase, half, v):
        return mz * 4 + v if phase == half else v * 4 + mx

    def mine(phase, half):
        return mx if phase == half else mz

    def place(half, j):
        v = mine(1, half)
        return (far(v), ahead(v), behind(v), v)[j]

    def weight(half, v, to, slot):
        def block(j):
            i = place(half, j)
            return (i * 4 + v) if half == 0 else (v * 4 + i)

        left_side = jnp.concatenate(
            [ogt[pl.ds(pl.multiple_of(block(i) * W, W), W), :] for i in range(4)], axis=0
        )

        def one(n, carry):
            at = pl.ds(pl.multiple_of(half * 512 + n * 256, 256), 256)
            value = dot(left_side, nm2[:, at])
            for i in range(4):
                to[slot, i, :, pl.ds(pl.multiple_of(n * 256, 256), 256)] = value[
                    i * W : (i + 1) * W
                ].astype(to.dtype)
            return carry

        lax.fori_loop(0, 2, one, 0)

    def phase1(slot, peer, part):
        at = pl.ds(2 * part, 2)
        return pltpu.make_async_remote_copy(
            src_ref=s1.at[slot, at],
            dst_ref=r1.at[slot, at],
            send_sem=r1_ss.at[2 * slot + part],
            recv_sem=r1_rs.at[2 * slot + part],
            device_id={"context": peer},
            device_id_type=MESH,
        )

    def phase2(slot, peer):
        return pltpu.make_async_remote_copy(
            src_ref=s2.at[slot],
            dst_ref=r2.at[slot],
            send_sem=r2_ss.at[slot],
            recv_sem=r2_rs.at[slot],
            device_id={"context": peer},
            device_id_type=MESH,
        )

    sends1, sends2 = [], []

    def start1(slot, peer, part):
        copy = phase1(slot, peer, part)
        copy.start()
        sends1.append(copy)

    def start2(slot, peer):
        copy = phase2(slot, peer)
        copy.start()
        sends2.append(copy)

    for half in range(2):
        v = mine(0, half)
        weight(half, far(v), s1, half)
        for part in range(2):
            start1(half, along(0, half, ahead(v)), part)

    project((myt + 2) % 4, False)
    acc2[...] = jnp.zeros_like(acc2)

    def norm_sums(q, carry):
        acc2[q // 4] += gn_s[:, lanes(q)] * gain_ref[:, lanes(q)] * ga_s[:, lanes(q)]
        return carry

    lax.fori_loop(0, NQ, norm_sums, 0)
    for g in range(2):
        inverse = invb[g]
        shift = jnp.sum(acc2[g], axis=1, keepdims=True) * (1.0 / 512)
        mub[g] = shift * inverse * inverse

    def norm_back(q, carry):
        g = q // 4
        gated = ga_s[:, lanes(q)]
        inverse = invb[g]
        gn = gn_s[:, lanes(q)]
        d_gated = inverse * (gn * gain_ref[:, lanes(q)] - gated * mub[g])
        rows[0, :, lanes(q)] = jnp.sum(gn * gated * inverse, axis=0, keepdims=True)
        xv = x_ref[:, lanes(q)].astype(F32)
        ssd = y_s[:, lanes(q)] + skx_s[:, lanes(q)]
        gg_v[:, lanes(q)] = (d_gated * ssd * bend_s[:, lanes(q)]).astype(BF)
        grad = d_gated * silu_s[:, lanes(q)]
        g_s[:, lanes(q)] = grad
        rows[1, :, lanes(q)] = jnp.sum(grad * xv, axis=0, keepdims=True)
        hi, lo = split2(eexp[:, lanes(q)] * grad)
        both = dot(qt[g], jnp.concatenate([hi, lo], axis=1))
        into = (both[:, :W] + both[:, W:]).astype(BF)
        bsnd[2 * q] = into[0:64]
        bsnd[2 * q + 1] = into[64:]
        return carry

    lax.fori_loop(0, NQ, norm_back, 0)
    send_all(bsnd, brcv, ba_ss, ba_rs)

    for half in range(2):
        weight(half, behind(mine(0, half)), s1, 2 + half)

    def send_behind(part):
        for half in range(2):
            start1(2 + half, along(0, half, behind(mine(0, half))), part)

    def relay1(part):
        for half in range(2):
            phase1(half, me, part).wait_recv()
            for i in (2 * part, 2 * part + 1):
                s1[4 + half, i] = (own1[2 + half, i] + r1[half, i].astype(F32)).astype(BF)
            start1(4 + half, along(0, half, ahead(mine(0, half))), part)

    for half in range(2):
        weight(half, ahead(mine(0, half)), own1, 2 + half)
    for half in range(2):
        weight(half, mine(0, half), own1, half)
    send_behind(0)
    relay1(0)
    brcv[me] = bsnd[me]
    recv_all(bsnd, brcv, ba_ss, ba_rs)
    run = jnp.zeros((64, W), F32)
    for s in range(CTX - 1, -1, -1):
        out_s[s] = run.astype(BF)
        run = brcv[s].astype(F32) + rcv[s, 64:65] * run
    send_all(out_s, outb, bb_ss, bb_rs)
    outb[me] = out_s[me]

    ds_s[...] = jnp.zeros_like(ds_s)
    dq_s[...] = jnp.zeros_like(dq_s)
    accr[...] = jnp.zeros_like(accr)
    accc[...] = jnp.zeros_like(accc)
    accv[...] = jnp.zeros_like(accv)

    def head_sums(q, value):
        row, lane = iota((NH, 2 * W), 0), iota((NH, 2 * W), 1) % W
        pick = (row == 2 * q + lane // 64).astype(BF)
        return dot_t(pick, jnp.concatenate(split2(value), axis=1))

    def within_back(q, carry):
        g = q // 4
        xp = x_ref[:, lanes(q)]
        grad = g_s[:, lanes(q)]
        ghi, glo = split2(grad)
        gthi, gtlo = ghi.T, glo.T
        x2 = jnp.concatenate([xp, xp], axis=1)
        zero = jnp.zeros((T, W), BF)
        parts = []
        total_ds = ds_s[g]
        for hh in range(2):
            h = 2 * q + hh
            keep = first if hh == 0 else jnp.logical_not(first)
            g2 = jnp.concatenate([jnp.where(keep, ghi, zero), jnp.where(keep, glo, zero)], axis=1)
            total_ds = total_ds + dot_t(g2, x2) * mt[h]
            a, b = gthi[64 * hh : 64 * hh + 64], gtlo[64 * hh : 64 * hh + 64]
            both = dot(jnp.concatenate([a, b], axis=0), phi[h])
            parts.append(both[0:64] + both[64:] + dot(a, plo[h]))
        ds_s[g] = total_ds
        dxw[:, lanes(q)] = jnp.concatenate(parts, axis=0).T
        accr[...] += head_sums(q, grad * y_s[:, lanes(q)])
        ehi, elo = split2(eexp[:, lanes(q)] * grad)
        shi, slo = split2(entering(q))
        to_q = dot_t(jnp.concatenate([ehi, elo], axis=1), jnp.concatenate([shi, shi], axis=1))
        dq_s[:, lanes(g)] += to_q + dot_t(ehi, slo)
        return carry

    lax.fori_loop(0, NQ, within_back, 0)
    send_behind(1)
    relay1(1)
    for g in range(2):
        hi, lo = split2(ds_s[g])
        kg = k_ref[:, g * W : (g + 1) * W]
        qg = q_ref[:, g * W : (g + 1) * W]
        dq_s[:, g * W : (g + 1) * W] += dot(hi, kg) + dot(lo, kg)
        dk_s[:, g * W : (g + 1) * W] = tdot(hi, qg) + tdot(lo, qg)

    def row_copy(src, dst, ss, rs, peer, slot):
        return pltpu.make_async_remote_copy(
            src_ref=src,
            dst_ref=dst.at[slot],
            send_sem=ss.at[peer],
            recv_sem=rs.at[slot],
            device_id={"context": peer},
            device_id_type=MESH,
        )

    def row_send(src, dst, ss, rs):
        def one(off, carry):
            row_copy(src, dst, ss, rs, (me + off) % CTX, me).start()
            return carry

        lax.fori_loop(1, CTX, one, 0)
        dst[me] = src[...]

    def row_sum(src, dst, ss, rs):
        def one(off, carry):
            row_copy(src, dst, ss, rs, (me + off) % CTX, (me + off) % CTX).wait_recv()
            return carry

        lax.fori_loop(1, CTX, one, 0)
        value = dst[0]
        for s in range(1, CTX):
            value = value + dst[s]
        return value

    def row_drain(src, dst, ss, rs):
        def one(off, carry):
            row_copy(src, dst, ss, rs, (me + off) % CTX, me).wait_send()
            return carry

        lax.fori_loop(1, CTX, one, 0)

    def as_row(column):
        at = iota((NH, W), 0) == iota((NH, W), 1)
        return jnp.sum(jnp.where(at, column, 0.0), axis=0, keepdims=True)

    ea_own[:, 0:C] = rows[0]
    ea_own[:, C : C + W] = as_row(per_head(rows[1]))
    row_send(ea_own, ea_rcv, ea_ss, ea_rs)

    recv_all(out_s, outb, bb_ss, bb_rs)

    def state_back(q, carry):
        g = q // 4
        d_state = jnp.concatenate([outb[2 * q], outb[2 * q + 1]], axis=0)
        rows[2, :, lanes(q)] = jnp.sum(
            d_state.astype(F32) * entering(q), axis=0, keepdims=True
        )
        weights = wexp[:, lanes(q)]
        xv = x_ref[:, lanes(q)].astype(F32)
        via = weights * dot(k_ref[:, lanes(g)], d_state)
        dx = dxw[:, lanes(q)] + via
        gi_v[:, lanes(q)] = (dx + rows[3, :, lanes(q)] * g_s[:, lanes(q)]).astype(BF)
        accc[...] += head_sums(q, xv * dx)
        accv[...] += head_sums(q, xv * via)
        whi, wlo = split2(weights * xv)
        twice = jnp.concatenate([d_state, d_state], axis=1)
        dk_s[:, lanes(g)] += dot_t(jnp.concatenate([whi, wlo], axis=1), twice)
        return carry

    lax.fori_loop(0, NQ, state_back, 0)

    raw = step_ref[...]
    slope = jnp.sum(jnp.where(eye, jnp.exp(rate_ref[...]), 0.0), axis=1, keepdims=True)
    step = stp_s[...]
    lower = (iota((T, T), 0) >= iota((T, T), 1)).astype(BF)
    after = dot3(accr[...] - accc[...], lower)
    log_grad = per_head(rows[2] * eexp[T - 1 : T, :])
    d_total = jnp.sum(accv[...], axis=1, keepdims=True) + log_grad
    d_decay = after + d_total
    gs_v[...] = (accc[...] / step - slope * d_decay) / (1.0 + jnp.exp(-raw))
    la_own[...] = as_row(jnp.sum(d_decay * (-slope * step), axis=1, keepdims=True))
    row_send(la_own, la_rcv, la_ss, la_rs)

    def await1(part):
        for slot in range(2, 6):
            phase1(slot, me, part).wait_recv()

    def summed(half, j):
        return own1[half, j] + r1[2 + half, j].astype(F32) + r1[4 + half, j].astype(F32)

    await1(0)
    for half in range(2):
        s2[half] = summed(half, 0).astype(BF)
        start2(half, along(1, half, ahead(mine(1, half))))
    for half in range(2):
        fwd2[half] = summed(half, 1)

    await1(1)
    for half in range(2):
        s2[2 + half] = summed(half, 2).astype(BF)
        start2(2 + half, along(1, half, behind(mine(1, half))))
    for half in range(2):
        gw_v[:, half * 512 : half * 512 + 512] = summed(half, 3)

    for half in range(2):
        phase2(half, me).wait_recv()
        s2[4 + half] = (fwd2[half] + r2[half].astype(F32)).astype(BF)
        start2(4 + half, along(1, half, ahead(mine(1, half))))
    ea_own2 = row_sum(ea_own, ea_rcv, ea_ss, ea_rs)
    row_drain(ea_own, ea_rcv, ea_ss, ea_rs)
    ea_own[...] = ea_own2
    pair_ea = pair(ea_own, ea_p, 3)
    pair_ea.start()
    drain_all(snd, rcv, fa_ss, fa_rs)
    drain_all(ent_s, ent, fb_ss, fb_rs)
    drain_all(bsnd, brcv, ba_ss, ba_rs)
    drain_all(out_s, outb, bb_ss, bb_rs)

    la_own2 = row_sum(la_own, la_rcv, la_ss, la_rs)
    row_drain(la_own, la_rcv, la_ss, la_rs)
    la_own[...] = la_own2
    pair_la = pair(la_own, la_p, 4)
    pair_la.start()
    pair_ea.wait()
    ea_own[...] += ea_p[...]
    pair_la.wait()
    la_own[...] += la_p[...]
    for copy in (*to_right, *to_left, relay_right, relay_left, pair_nm, *sends1):
        copy.wait_send()
    for i in range(2):
        pair_og(2 * other + i).wait_send()
    for half in range(2):
        at = slice(half * 512, half * 512 + 512)
        phase2(2 + half, me).wait_recv()
        gw_v[:, at] += r2[2 + half].astype(F32)
    for half in range(2):
        at = slice(half * 512, half * 512 + 512)
        phase2(4 + half, me).wait_recv()
        gw_v[:, at] += r2[4 + half].astype(F32)
    for copy in sends2:
        copy.wait_send()


def hand_out(
    gi_v, gg_v, gk_v, gq_v, gs_v, gw_v, early_v, late_v,
    gi_out, gg_out, gk_out, gq_out, gs_out, gw_out, rate_ref, skip_ref, norm_ref, out_sem,
):
    ways = (
        (gi_v, gi_out), (gg_v, gg_out), (gw_v, gw_out), (gk_v, gk_out), (gq_v, gq_out),
        (gs_v, gs_out),
    )
    out = [pltpu.make_async_copy(*way, out_sem.at[i]) for i, way in enumerate(ways)]
    for copy in out:
        copy.start()
    norm_ref[...] = early_v[:, 0:C]
    skip_ref[...] = early_v[:, C : C + NH]
    rate_ref[...] = late_v[:, 0:NH]
    for copy in out:
        copy.wait()


def body(
    ssm_input, gate_input, state_keys, state_queries, step_raw,
    rate_log, skip_gain, norm_gain, out_weight, out_grad,
):
    vmem, anywhere = pl.BlockSpec(memory_space=pltpu.VMEM), pl.BlockSpec(memory_space=pl.ANY)
    V, S = pltpu.VMEM, pltpu.SemaphoreType.DMA
    shape = jax.ShapeDtypeStruct
    wide, by_pos, per_ctx = V((T, C), F32), V((2, T, W), F32), V((CTX, 64, W), BF)
    scratch = [
        V((T, C), BF), V((T, 2 * W), BF), V((T, 2 * W), BF), V((NH, T), F32), V((1, NH), F32),
        V((1, NH), F32), V((1, C), F32),
        V((T, C), BF), V((4 * C, C), BF), V((4, T, C), BF), V((2, T, C), BF), V((2 * C, 2 * T), BF),
        V((2 * T, C), BF),
        wide, wide, wide, V((NH, T), F32), V((NH, T), F32), V((2, W, T), BF), V((2, W, T), BF),
        V((2, T, T), F32),
        V((CTX, 72, W), F32), V((CTX, 72, W), F32), V((CTX, 64, W), F32), V((CTX, 64, W), F32),
        per_ctx, per_ctx, per_ctx, per_ctx,
        wide, wide, wide, V((NH, T, T), F32), V((NH, T, T), BF), V((NH, T, T), BF),
        wide, wide, wide, wide, by_pos, by_pos, by_pos, by_pos,
        V((2, T, T), F32), wide,
        V((4, 1, C), F32), V((NH, T), F32), V((NH, T), F32), V((NH, T), F32),
        V((CTX, 1, C + W), F32), V((1, C + W), F32), V((CTX, 1, W), F32), V((1, W), F32),
        V((6, 4, W, 512), BF), V((6, 4, W, 512), BF), V((4, 4, W, 512), F32),
        V((6, W, 512), BF), V((6, W, 512), BF), V((2, W, 512), F32),
        S((10,)), S((6,)), S((6,)), *[S((CTX,))] * 8,
        S((5,)), S((5,)), S((12,)), S((12,)), S((6,)), S((6,)), *[S((CTX,))] * 4,
    ]
    parts = pl.pallas_call(
        kernel,
        out_shape=(
            V((T, C), BF), V((T, C), BF), V((T, 2 * W), F32), V((T, 2 * W), F32),
            V((NH, T), F32), V((W, C), F32), V((1, C + W), F32), V((1, W), F32),
        ),
        in_specs=[anywhere] * 10,
        out_specs=[vmem] * 8,
        scratch_shapes=scratch,
        compiler_params=pltpu.CompilerParams(
            collective_id=0, has_side_effects=True, vmem_limit_bytes=60 * 1024 * 1024
        ),
    )(
        ssm_input[0], state_keys[0], state_queries[0], step_raw[0],
        rate_log.reshape(1, NH), skip_gain.reshape(1, NH), norm_gain.reshape(1, C),
        gate_input[0], out_weight, out_grad[0],
    )
    gi, gg, gk, gq, gs, gw, rate, skip, norm = pl.pallas_call(
        hand_out,
        out_shape=(
            shape((T, C), BF), shape((T, C), BF), shape((T, 2 * W), F32), shape((T, 2 * W), F32),
            shape((NH, T), F32), shape((W, C), F32),
            shape((1, NH), F32), shape((1, NH), F32), shape((1, C), F32),
        ),
        in_specs=[vmem] * 8,
        out_specs=[anywhere] * 6 + [vmem] * 3,
        scratch_shapes=[S((6,))],
    )(*[pltpu.with_memory_space_constraint(p, pltpu.VMEM) for p in parts])
    return (
        gi[None], gg[None], gk[None], gq[None], gs[None],
        rate.reshape(NH), skip.reshape(NH), norm.reshape(C), gw,
    )


def solution(mesh):
    return jax.shard_map(
        body,
        mesh=mesh,
        in_specs=(
            P("dp", "context", "tensor"),
            P("dp", "context", "tensor"),
            P("dp", "context", "tensor"),
            P("dp", "context", "tensor"),
            P("dp", "tensor", "context"),
            P("tensor"),
            P("tensor"),
            P("tensor"),
            P(None, "tensor"),
            P("dp", "context", "tensor"),
        ),
        out_specs=(
            P("dp", "context", "tensor"),
            P("dp", "context", "tensor"),
            P("dp", "context", "tensor"),
            P("dp", "context", "tensor"),
            P("dp", "tensor", "context"),
            P("tensor"),
            P("tensor"),
            P("tensor"),
            P(("dp", "context"), "tensor"),
        ),
        check_vma=False,
    )
```

```python
import jax
import jax.numpy as jnp
from jax import lax
from jax.experimental import pallas as pl
from jax.experimental.pallas import tpu as pltpu
from jax.sharding import PartitionSpec as P

F32 = jnp.float32
BF = jnp.bfloat16
EPSILON = 1e-05
MESH = pl.DeviceIdType.MESH

T = 256
C = 1024
NH = 16
NQ = 8
W = 128
CTX = 16


def dot(a, b):
    return lax.dot_general(a, b, (((1,), (0,)), ((), ())), preferred_element_type=F32)


def dot_t(a, b):
    return lax.dot_general(a, b, (((1,), (1,)), ((), ())), preferred_element_type=F32)


def tdot(a, b):
    return lax.dot_general(a, b, (((0,), (0,)), ((), ())), preferred_element_type=F32)


def split2(v):
    hi = v.astype(BF)
    return hi, (v - hi.astype(F32)).astype(BF)


def split3(v):
    hi = v.astype(BF)
    rest = v - hi.astype(F32)
    mid = rest.astype(BF)
    return hi, mid, (rest - mid.astype(F32)).astype(BF)


def dot3(v, ones):
    parts = dot(jnp.concatenate(split3(v), axis=0), ones)
    return parts[0:NH] + parts[NH : 2 * NH] + parts[2 * NH : 3 * NH]


def iota(shape, axis):
    return lax.broadcasted_iota(jnp.int32, shape, axis)


def lanes(q):
    return pl.ds(pl.multiple_of(q * W, W), W)


def per_head(row):
    own = (iota((NH, C), 1) // 64) == iota((NH, C), 0)
    return jnp.sum(jnp.where(own, row, 0.0), axis=1, keepdims=True)


def kernel(
    x_hbm, k_hbm, q_hbm, step_hbm, rate_hbm, skip_hbm, gain_hbm, gate_hbm, w_hbm, og_hbm,
    gi_v, gg_v, dk_s, dq_s, gs_v, gw_v, ea_own, la_own,
    x_ref, k_ref, q_ref, step_ref, rate_ref, skip_ref, gain_ref,
    gate_v, w_v, ogf, ogp, ogt, nm2,
    cumx, eexp, wexp, cum_s, stp_s, kt, qt, sc,
    snd, rcv, ent_s, ent, bsnd, brcv, out_s, outb,
    silu_s, bend_s, skx_s, mt, phi, plo, y_s, gn_s, ga_s, g_s, acc, acc2, invb, mub,
    ds_s, dxw, rows, accr, accc, accv,
    ea_rcv, ea_p, la_rcv, la_p, s1, r1, own1, s2, r2,
    in_sem, og_ss, og_rs, leg_ss, leg_rs, p_ss, p_rs, r1_ss, r1_rs, r2_ss, r2_rs,
):
    me = lax.axis_index("context")
    myt = lax.axis_index("tensor")
    mydp = lax.axis_index("dp")
    mz, mx = me // 4, me % 4
    other = 1 - mydp
    right, left = (myt + 1) % 4, (myt + 3) % 4

    barrier = pltpu.get_barrier_semaphore()

    def greet(off, carry):
        pl.semaphore_signal(
            barrier, inc=1, device_id={"context": (me + off) % CTX}, device_id_type=MESH
        )
        return carry

    pl.semaphore_signal(barrier, inc=1, device_id={"tensor": right}, device_id_type=MESH)
    pl.semaphore_signal(barrier, inc=1, device_id={"tensor": left}, device_id_type=MESH)
    lax.fori_loop(1, CTX, greet, 0)
    pl.semaphore_signal(barrier, inc=1, device_id={"dp": other}, device_id_type=MESH)

    loads = [
        pltpu.make_async_copy(src, dst, in_sem.at[i])
        for i, (src, dst) in enumerate(
            (
                (step_hbm, step_ref), (rate_hbm, rate_ref), (skip_hbm, skip_ref), (k_hbm, k_ref),
                (x_hbm, x_ref), (q_hbm, q_ref), (gain_hbm, gain_ref), (og_hbm, ogf.at[myt]),
                (gate_hbm, gate_v), (w_hbm, w_v),
            )
        )
    ]
    for copy in loads:
        copy.start()
    for copy in loads[:3]:
        copy.wait()

    raw = step_ref[...]
    eye = iota((NH, NH), 0) == iota((NH, NH), 1)
    slope = jnp.sum(jnp.where(eye, jnp.exp(rate_ref[...]), 0.0), axis=1, keepdims=True)
    step = jnp.maximum(raw, 0.0) + jnp.log(1.0 + jnp.exp(-jnp.abs(raw)))
    decay = -slope * step
    upper = (iota((T, T), 0) <= iota((T, T), 1)).astype(BF)
    cum = dot3(decay, upper)
    total = cum[:, T - 1 : T]
    stp_s[...] = step
    cum_s[...] = cum
    spread = ((iota((3 * NH, C), 0) % NH) == (iota((3 * NH, C), 1) // 64)).astype(BF)

    def expand(v, to):
        pieces = jnp.concatenate(split3(v), axis=0).astype(F32)
        turned = jnp.concatenate([pieces, jnp.zeros((W - 3 * NH, T), F32)], axis=0).T
        to[...] = dot(turned[:, : 3 * NH].astype(BF), spread)

    expand(jnp.exp(total - cum) * step, wexp)
    expand(jnp.exp(cum), eexp)
    own = (iota((NH, C), 1) // 64) == iota((NH, C), 0)
    skip_col = jnp.sum(jnp.where(eye, skip_ref[...], 0.0), axis=1, keepdims=True)
    rows[3] = jnp.sum(jnp.where(own, skip_col, 0.0), axis=0, keepdims=True)

    loads[3].wait()
    for g in range(2):
        kt[g] = k_ref[:, g * W : (g + 1) * W].T
    loads[4].wait()

    def local_state(q, carry):
        hi, lo = split2(x_ref[:, lanes(q)].astype(F32) * wexp[:, lanes(q)])
        both = dot(kt[q // 4], jnp.concatenate([hi, lo], axis=1))
        state = both[:, :W] + both[:, W:]
        factor = jnp.broadcast_to(eexp[T - 1 : T, lanes(q)], (8, W))
        snd[2 * q, 0:64] = state[0:64]
        snd[2 * q + 1, 0:64] = state[64:]
        snd[2 * q, 64:72] = factor
        snd[2 * q + 1, 64:72] = factor
        return carry

    lax.fori_loop(0, NQ, local_state, 0)

    pl.semaphore_wait(barrier, CTX + 2)

    def send_all(src, dst, leg):
        def one(off, carry):
            peer = (me + off) % CTX
            pltpu.make_async_remote_copy(
                src_ref=src.at[peer],
                dst_ref=dst.at[me],
                send_sem=leg_ss.at[leg],
                recv_sem=leg_rs.at[leg],
                device_id={"context": peer},
                device_id_type=MESH,
            ).start()
            return carry

        lax.fori_loop(1, CTX, one, 0)

    def all_of(slots, leg):
        some = slots.at[pl.ds(0, CTX - 1)]
        return pltpu.make_async_remote_copy(
            src_ref=some,
            dst_ref=some,
            send_sem=leg_ss.at[leg],
            recv_sem=leg_rs.at[leg],
            device_id={"context": (me + 1) % CTX},
            device_id_type=MESH,
        )

    def ring(src, dst, sem, peer):
        return pltpu.make_async_remote_copy(
            src_ref=src,
            dst_ref=dst,
            send_sem=og_ss.at[0],
            recv_sem=og_rs.at[sem],
            device_id={"tensor": peer},
            device_id_type=MESH,
        )

    top, low = pl.ds(0, 128), pl.ds(128, 128)
    to_right = [ring(og_hbm.at[h], ogf.at[myt, h], i, right) for i, h in enumerate((top, low))]
    to_left = [ring(og_hbm.at[h], ogf.at[myt, h], 2 + i, left) for i, h in enumerate((low, top))]
    to_right[0].start()
    to_left[0].start()
    send_all(snd, rcv, 0)

    to_right[1].start()
    to_left[1].start()

    expand(cum_s[...], cumx)
    loads[5].wait()
    for g in range(2):
        qg = q_ref[:, g * W : (g + 1) * W]
        qt[g] = qg.T
        sc[g] = dot_t(qg, k_ref[:, g * W : (g + 1) * W])
    causal = iota((T, T), 0) >= iota((T, T), 1)
    first = iota((T, W), 1) < 64

    def within(q, carry):
        xp = x_ref[:, lanes(q)]
        spread_tile = cumx[:, lanes(q)]
        outs = []
        for hh in range(2):
            h = 2 * q + hh
            column = spread_tile[:, 64 * hh : 64 * hh + 1]
            gap = column - cum_s[pl.ds(h, 1), :]
            m = jnp.exp(jnp.where(causal, gap, -1e30)) * stp_s[pl.ds(h, 1), :]
            mt[h] = m
            hi, lo = split2(m * sc[q // 4])
            phi[h] = hi
            plo[h] = lo
            outs.append(dot(hi, xp) + dot(lo, xp))
        y_s[:, lanes(q)] = jnp.where(first, outs[0], outs[1])
        return carry

    lax.fori_loop(0, NQ, within, 0)

    rcv[me] = snd[me]
    all_of(rcv, 0).wait_recv()
    run = jnp.zeros((64, W), F32)
    for s in range(CTX):
        ent_s[s] = run
        run = rcv[s, 64:65] * run + rcv[s, 0:64]
    send_all(ent_s, ent, 1)
    ent[me] = ent_s[me]

    to_right[0].wait_recv()
    relay_right = ring(ogf.at[left, top], ogf.at[left, top], 4, right)
    relay_right.start()
    to_left[0].wait_recv()
    relay_left = ring(ogf.at[right, low], ogf.at[right, low], 4, left)
    relay_left.start()
    loads[8].wait()

    def gates(q, carry):
        gate = gate_v[:, lanes(q)].astype(F32)
        sig = 1.0 / (1.0 + jnp.exp(-gate))
        silu = gate * sig
        silu_s[:, lanes(q)] = silu
        bend_s[:, lanes(q)] = sig * (1.0 + gate - silu)
        skx_s[:, lanes(q)] = rows[3, :, lanes(q)] * x_ref[:, lanes(q)].astype(F32)
        return carry

    lax.fori_loop(0, NQ, gates, 0)

    loads[7].wait()
    loads[9].wait()

    def pair(src, dst, sem):
        return pltpu.make_async_remote_copy(
            src_ref=src,
            dst_ref=dst,
            send_sem=p_ss.at[sem],
            recv_sem=p_rs.at[sem],
            device_id={"dp": other},
            device_id_type=MESH,
        )

    def pair_og(chunk):
        return pair(ogf.at[chunk], ogp.at[chunk % 2], chunk % 2)

    def hand_over(chunk):
        @pl.when(chunk // 2 == other)
        def _():
            pair_og(chunk).start()

        @pl.when(chunk // 2 == mydp)
        def _():
            def turn(i, carry):
                at = pl.ds(pl.multiple_of((chunk % 2) * C + i * W, W), W)
                ogt[at, 0:T] = ogf[chunk, :, lanes(i)].T
                return carry

            lax.fori_loop(0, 8, turn, 0)

    def project(chunk, first_term):
        def one(n, carry):
            where = pl.ds(pl.multiple_of(n * 256, 256), 256)
            part = dot(ogf[chunk], w_v[pl.ds(pl.multiple_of(chunk * C, C), C), where])
            gn_s[:, where] = part if first_term else gn_s[:, where] + part
            return carry

        lax.fori_loop(0, 4, one, 0)

    def take(chunk, first_term):
        hand_over(chunk)
        project(chunk, first_term)

    def turn_pair(chunk):
        @pl.when(chunk // 2 == mydp)
        def _():
            pair_og(chunk).wait_recv()

            def turn(i, carry):
                at = pl.ds(pl.multiple_of((chunk % 2) * C + i * W, W), W)
                ogt[at, T : 2 * T] = ogp[chunk % 2, :, lanes(i)].T
                return carry

            lax.fori_loop(0, 8, turn, 0)

    take(myt, True)
    loads[6].wait()
    to_right[1].wait_recv()
    to_left[1].wait_recv()
    hand_over(left)
    hand_over(right)
    turn_pair(myt)
    project(left, False)
    turn_pair(left)
    turn_pair(right)
    all_of(ent, 1).wait_recv()

    acc[...] = jnp.zeros_like(acc)

    def entering(q):
        return jnp.concatenate([ent[2 * q], ent[2 * q + 1]], axis=0)

    def group_q(q):
        return q_ref[:, lanes(q // 4)]

    def scan_out(q, carry):
        g = q // 4
        twice = jnp.concatenate([group_q(q), group_q(q)], axis=1)
        carried = dot(twice, jnp.concatenate(split2(entering(q)), axis=0))
        y = y_s[:, lanes(q)] + eexp[:, lanes(q)] * carried
        y_s[:, lanes(q)] = y
        gated = (y + skx_s[:, lanes(q)]) * silu_s[:, lanes(q)]
        ga_s[:, lanes(q)] = gated
        acc[g] += gated * gated
        return carry

    lax.fori_loop(0, NQ, scan_out, 0)
    for g in range(2):
        mean = jnp.sum(acc[g], axis=1, keepdims=True) * (1.0 / 512)
        invb[g] = jnp.broadcast_to(lax.rsqrt(mean + EPSILON), (T, W))

    def normalize(q, carry):
        value = ga_s[:, lanes(q)] * invb[q // 4] * gain_ref[:, lanes(q)]
        nm2[0:T, lanes(q)] = value.astype(BF)
        return carry

    lax.fori_loop(0, NQ, normalize, 0)
    pair_nm = pair(nm2.at[0:T], nm2.at[T : 2 * T], 2)
    pair_nm.start()

    ring(ogf.at[0], ogf.at[0], 4, right).wait_recv()
    hand_over((myt + 2) % 4)
    project(right, False)
    turn_pair((myt + 2) % 4)
    pair_nm.wait_recv()

    def ahead(v):
        return (v + 1 + 2 * mydp) % 4

    def behind(v):
        return (v + 3 - 2 * mydp) % 4

    def far(v):
        return (v + 2) % 4

    def along(phase, half, v):
        return mz * 4 + v if phase == half else v * 4 + mx

    def mine(phase, half):
        return mx if phase == half else mz

    def place(half, j):
        v = mine(1, half)
        return (far(v), ahead(v), behind(v), v)[j]

    def weight(half, v, to, slot):
        def block(j):
            i = place(half, j)
            return (i * 4 + v) if half == 0 else (v * 4 + i)

        left_side = jnp.concatenate(
            [ogt[pl.ds(pl.multiple_of(block(i) * W, W), W), :] for i in range(4)], axis=0
        )

        def one(n, carry):
            at = pl.ds(pl.multiple_of(half * 512 + n * 256, 256), 256)
            value = dot(left_side, nm2[:, at])
            for i in range(4):
                to[slot, i, :, pl.ds(pl.multiple_of(n * 256, 256), 256)] = value[
                    i * W : (i + 1) * W
                ].astype(to.dtype)
            return carry

        lax.fori_loop(0, 2, one, 0)

    def phase1(slot, peer, part):
        at = pl.ds(2 * part, 2)
        return pltpu.make_async_remote_copy(
            src_ref=s1.at[slot, at],
            dst_ref=r1.at[slot, at],
            send_sem=r1_ss.at[0],
            recv_sem=r1_rs.at[part if slot > 1 else 2 + 2 * slot + part],
            device_id={"context": peer},
            device_id_type=MESH,
        )

    def phase2(slot, peer):
        return pltpu.make_async_remote_copy(
            src_ref=s2.at[slot],
            dst_ref=r2.at[slot],
            send_sem=r2_ss.at[0],
            recv_sem=r2_rs.at[0],
            device_id={"context": peer},
            device_id_type=MESH,
        )

    def start1(slot, peer, part):
        phase1(slot, peer, part).start()

    def start2(slot, peer):
        phase2(slot, peer).start()

    def every1(ref, sem):
        return pltpu.make_async_remote_copy(
            src_ref=s1,
            dst_ref=ref,
            send_sem=r1_ss.at[0],
            recv_sem=r1_rs.at[sem],
            device_id={"context": (me + 1) % CTX},
            device_id_type=MESH,
        )

    every2 = pltpu.make_async_remote_copy(
        src_ref=s2,
        dst_ref=r2,
        send_sem=r2_ss.at[0],
        recv_sem=r2_rs.at[0],
        device_id={"context": (me + 1) % CTX},
        device_id_type=MESH,
    )

    for half in range(2):
        v = mine(0, half)
        weight(half, far(v), s1, half)
        for part in range(2):
            start1(half, along(0, half, ahead(v)), part)

    project((myt + 2) % 4, False)
    acc2[...] = jnp.zeros_like(acc2)

    def norm_sums(q, carry):
        acc2[q // 4] += gn_s[:, lanes(q)] * gain_ref[:, lanes(q)] * ga_s[:, lanes(q)]
        return carry

    lax.fori_loop(0, NQ, norm_sums, 0)
    for g in range(2):
        inverse = invb[g]
        shift = jnp.sum(acc2[g], axis=1, keepdims=True) * (1.0 / 512)
        mub[g] = shift * inverse * inverse

    def norm_back(q, carry):
        g = q // 4
        gated = ga_s[:, lanes(q)]
        inverse = invb[g]
        gn = gn_s[:, lanes(q)]
        d_gated = inverse * (gn * gain_ref[:, lanes(q)] - gated * mub[g])
        rows[0, :, lanes(q)] = jnp.sum(gn * gated * inverse, axis=0, keepdims=True)
        xv = x_ref[:, lanes(q)].astype(F32)
        ssd = y_s[:, lanes(q)] + skx_s[:, lanes(q)]
        gg_v[:, lanes(q)] = (d_gated * ssd * bend_s[:, lanes(q)]).astype(BF)
        grad = d_gated * silu_s[:, lanes(q)]
        g_s[:, lanes(q)] = grad
        rows[1, :, lanes(q)] = jnp.sum(grad * xv, axis=0, keepdims=True)
        hi, lo = split2(eexp[:, lanes(q)] * grad)
        both = dot(qt[g], jnp.concatenate([hi, lo], axis=1))
        into = (both[:, :W] + both[:, W:]).astype(BF)
        bsnd[2 * q] = into[0:64]
        bsnd[2 * q + 1] = into[64:]
        return carry

    lax.fori_loop(0, NQ, norm_back, 0)
    send_all(bsnd, brcv, 2)

    for half in range(2):
        weight(half, behind(mine(0, half)), s1, 2 + half)

    def send_behind(part):
        for half in range(2):
            start1(2 + half, along(0, half, behind(mine(0, half))), part)

    def relay1(part):
        for half in range(2):
            phase1(half, me, part).wait_recv()
            for i in (2 * part, 2 * part + 1):
                s1[4 + half, i] = (own1[2 + half, i] + r1[half, i].astype(F32)).astype(BF)
            start1(4 + half, along(0, half, ahead(mine(0, half))), part)

    for half in range(2):
        weight(half, ahead(mine(0, half)), own1, 2 + half)
    for half in range(2):
        weight(half, mine(0, half), own1, half)
    send_behind(0)
    relay1(0)
    brcv[me] = bsnd[me]
    all_of(brcv, 2).wait_recv()
    run = jnp.zeros((64, W), F32)
    for s in range(CTX - 1, -1, -1):
        out_s[s] = run.astype(BF)
        run = brcv[s].astype(F32) + rcv[s, 64:65] * run
    send_all(out_s, outb, 3)
    outb[me] = out_s[me]

    ds_s[...] = jnp.zeros_like(ds_s)
    dq_s[...] = jnp.zeros_like(dq_s)
    accr[...] = jnp.zeros_like(accr)
    accc[...] = jnp.zeros_like(accc)
    accv[...] = jnp.zeros_like(accv)

    def head_sums(q, value):
        row, lane = iota((NH, 2 * W), 0), iota((NH, 2 * W), 1) % W
        pick = (row == 2 * q + lane // 64).astype(BF)
        return dot_t(pick, jnp.concatenate(split2(value), axis=1))

    def within_back(q, carry):
        g = q // 4
        xp = x_ref[:, lanes(q)]
        grad = g_s[:, lanes(q)]
        ghi, glo = split2(grad)
        gthi, gtlo = ghi.T, glo.T
        x2 = jnp.concatenate([xp, xp], axis=1)
        zero = jnp.zeros((T, W), BF)
        parts = []
        total_ds = ds_s[g]
        for hh in range(2):
            h = 2 * q + hh
            keep = first if hh == 0 else jnp.logical_not(first)
            g2 = jnp.concatenate([jnp.where(keep, ghi, zero), jnp.where(keep, glo, zero)], axis=1)
            total_ds = total_ds + dot_t(g2, x2) * mt[h]
            a, b = gthi[64 * hh : 64 * hh + 64], gtlo[64 * hh : 64 * hh + 64]
            both = dot(jnp.concatenate([a, b], axis=0), phi[h])
            parts.append(both[0:64] + both[64:] + dot(a, plo[h]))
        ds_s[g] = total_ds
        dxw[:, lanes(q)] = jnp.concatenate(parts, axis=0).T
        accr[...] += head_sums(q, grad * y_s[:, lanes(q)])
        ehi, elo = split2(eexp[:, lanes(q)] * grad)
        shi, slo = split2(entering(q))
        to_q = dot_t(jnp.concatenate([ehi, elo], axis=1), jnp.concatenate([shi, shi], axis=1))
        dq_s[:, lanes(g)] += to_q + dot_t(ehi, slo)
        return carry

    lax.fori_loop(0, NQ, within_back, 0)
    send_behind(1)
    relay1(1)
    for g in range(2):
        hi, lo = split2(ds_s[g])
        kg = k_ref[:, g * W : (g + 1) * W]
        qg = q_ref[:, g * W : (g + 1) * W]
        dq_s[:, g * W : (g + 1) * W] += dot(hi, kg) + dot(lo, kg)
        dk_s[:, g * W : (g + 1) * W] = tdot(hi, qg) + tdot(lo, qg)

    def row_send(src, dst, leg):
        def one(off, carry):
            peer = (me + off) % CTX
            pltpu.make_async_remote_copy(
                src_ref=src,
                dst_ref=dst.at[me],
                send_sem=leg_ss.at[leg],
                recv_sem=leg_rs.at[leg],
                device_id={"context": peer},
                device_id_type=MESH,
            ).start()
            return carry

        lax.fori_loop(1, CTX, one, 0)
        dst[me] = src[...]

    def row_sum(src, dst, leg):
        all_of(dst, leg).wait_recv()
        value = dst[0]
        for i in range(1, CTX):
            value = value + dst[i]
        all_of(dst, leg).wait_send()
        src[...] = value

    def as_row(column):
        at = iota((NH, W), 0) == iota((NH, W), 1)
        return jnp.sum(jnp.where(at, column, 0.0), axis=0, keepdims=True)

    ea_own[:, 0:C] = rows[0]
    ea_own[:, C : C + W] = as_row(per_head(rows[1]))
    row_send(ea_own, ea_rcv, 4)

    all_of(outb, 3).wait_recv()

    def state_back(q, carry):
        g = q // 4
        d_state = jnp.concatenate([outb[2 * q], outb[2 * q + 1]], axis=0)
        rows[2, :, lanes(q)] = jnp.sum(
            d_state.astype(F32) * entering(q), axis=0, keepdims=True
        )
        weights = wexp[:, lanes(q)]
        xv = x_ref[:, lanes(q)].astype(F32)
        via = weights * dot(k_ref[:, lanes(g)], d_state)
        dx = dxw[:, lanes(q)] + via
        gi_v[:, lanes(q)] = (dx + rows[3, :, lanes(q)] * g_s[:, lanes(q)]).astype(BF)
        accc[...] += head_sums(q, xv * dx)
        accv[...] += head_sums(q, xv * via)
        whi, wlo = split2(weights * xv)
        twice = jnp.concatenate([d_state, d_state], axis=1)
        dk_s[:, lanes(g)] += dot_t(jnp.concatenate([whi, wlo], axis=1), twice)
        return carry

    lax.fori_loop(0, NQ, state_back, 0)

    raw = step_ref[...]
    slope = jnp.sum(jnp.where(eye, jnp.exp(rate_ref[...]), 0.0), axis=1, keepdims=True)
    step = stp_s[...]
    lower = (iota((T, T), 0) >= iota((T, T), 1)).astype(BF)
    after = dot3(accr[...] - accc[...], lower)
    log_grad = per_head(rows[2] * eexp[T - 1 : T, :])
    d_total = jnp.sum(accv[...], axis=1, keepdims=True) + log_grad
    d_decay = after + d_total
    gs_v[...] = (accc[...] / step - slope * d_decay) / (1.0 + jnp.exp(-raw))
    la_own[...] = as_row(jnp.sum(d_decay * (-slope * step), axis=1, keepdims=True))
    row_send(la_own, la_rcv, 5)

    def await1(part):
        every1(r1.at[pl.ds(2, 4), pl.ds(2 * part, 2)], part).wait_recv()

    def summed(half, j):
        return own1[half, j] + r1[2 + half, j].astype(F32) + r1[4 + half, j].astype(F32)

    await1(0)
    for half in range(2):
        v = mine(1, half)
        for j, there in ((0, far(v)), (1, ahead(v))):
            s2[2 * j + half] = summed(half, j).astype(BF)
            start2(2 * j + half, along(1, half, there))

    await1(1)
    for half in range(2):
        s2[4 + half] = summed(half, 2).astype(BF)
        start2(4 + half, along(1, half, behind(mine(1, half))))
    for half in range(2):
        gw_v[:, half * 512 : half * 512 + 512] = summed(half, 3)

    row_sum(la_own, la_rcv, 5)
    pair_la = pair(la_own, la_p, 4)
    pair_la.start()
    row_sum(ea_own, ea_rcv, 4)
    pair_ea = pair(ea_own, ea_p, 3)
    pair_ea.start()
    all_of(rcv, 0).wait_send()
    all_of(ent, 1).wait_send()
    all_of(brcv, 2).wait_send()
    all_of(outb, 3).wait_send()

    pair_ea.wait()
    ea_own[...] += ea_p[...]
    pair_la.wait()
    la_own[...] += la_p[...]
    ring(ogf.at[pl.ds(0, 3)], ogf.at[pl.ds(0, 3)], 4, right).wait_send()
    pair_nm.wait_send()
    every1(r1, 0).wait_send()
    for i in range(2):
        pair_og(2 * other + i).wait_send()
    every2.wait_recv()
    for half in range(2):
        at = slice(half * 512, half * 512 + 512)
        gw_v[:, at] += (
            r2[half].astype(F32) + r2[2 + half].astype(F32) + r2[4 + half].astype(F32)
        )
    every2.wait_send()


def hand_out(
    gi_v, gg_v, gk_v, gq_v, gs_v, gw_v, early_v, late_v,
    gi_out, gg_out, gk_out, gq_out, gs_out, gw_out, rate_ref, skip_ref, norm_ref, out_sem,
):
    ways = (
        (gi_v, gi_out), (gg_v, gg_out), (gw_v, gw_out), (gk_v, gk_out), (gq_v, gq_out),
        (gs_v, gs_out),
    )
    out = [pltpu.make_async_copy(*way, out_sem.at[i]) for i, way in enumerate(ways)]
    for copy in out:
        copy.start()
    norm_ref[...] = early_v[:, 0:C]
    skip_ref[...] = early_v[:, C : C + NH]
    rate_ref[...] = late_v[:, 0:NH]
    for copy in out:
        copy.wait()


def body(
    ssm_input, gate_input, state_keys, state_queries, step_raw,
    rate_log, skip_gain, norm_gain, out_weight, out_grad,
):
    vmem, anywhere = pl.BlockSpec(memory_space=pltpu.VMEM), pl.BlockSpec(memory_space=pl.ANY)
    V, S = pltpu.VMEM, pltpu.SemaphoreType.DMA
    shape = jax.ShapeDtypeStruct
    wide, by_pos, per_ctx = V((T, C), F32), V((2, T, W), F32), V((CTX, 64, W), BF)
    scratch = [
        V((T, C), BF), V((T, 2 * W), BF), V((T, 2 * W), BF), V((NH, T), F32), V((1, NH), F32),
        V((1, NH), F32), V((1, C), F32),
        V((T, C), BF), V((4 * C, C), BF), V((4, T, C), BF), V((2, T, C), BF), V((2 * C, 2 * T), BF),
        V((2 * T, C), BF),
        wide, wide, wide, V((NH, T), F32), V((NH, T), F32), V((2, W, T), BF), V((2, W, T), BF),
        V((2, T, T), F32),
        V((CTX, 72, W), F32), V((CTX, 72, W), F32), V((CTX, 64, W), F32), V((CTX, 64, W), F32),
        per_ctx, per_ctx, per_ctx, per_ctx,
        wide, wide, wide, V((NH, T, T), F32), V((NH, T, T), BF), V((NH, T, T), BF),
        wide, wide, wide, wide, by_pos, by_pos, by_pos, by_pos,
        V((2, T, T), F32), wide,
        V((4, 1, C), F32), V((NH, T), F32), V((NH, T), F32), V((NH, T), F32),
        V((CTX, 1, C + W), F32), V((1, C + W), F32), V((CTX, 1, W), F32), V((1, W), F32),
        V((6, 4, W, 512), BF), V((6, 4, W, 512), BF), V((4, 4, W, 512), F32),
        V((6, W, 512), BF), V((6, W, 512), BF),
        S((10,)), S((1,)), S((5,)), S((6,)), S((6,)),
        S((5,)), S((5,)), S((1,)), S((6,)), S((1,)), S((1,)),
    ]
    parts = pl.pallas_call(
        kernel,
        out_shape=(
            V((T, C), BF), V((T, C), BF), V((T, 2 * W), F32), V((T, 2 * W), F32),
            V((NH, T), F32), V((W, C), F32), V((1, C + W), F32), V((1, W), F32),
        ),
        in_specs=[anywhere] * 10,
        out_specs=[vmem] * 8,
        scratch_shapes=scratch,
        compiler_params=pltpu.CompilerParams(
            collective_id=0, has_side_effects=True, vmem_limit_bytes=60 * 1024 * 1024
        ),
    )(
        ssm_input[0], state_keys[0], state_queries[0], step_raw[0],
        rate_log.reshape(1, NH), skip_gain.reshape(1, NH), norm_gain.reshape(1, C),
        gate_input[0], out_weight, out_grad[0],
    )
    gi, gg, gk, gq, gs, gw, rate, skip, norm = pl.pallas_call(
        hand_out,
        out_shape=(
            shape((T, C), BF), shape((T, C), BF), shape((T, 2 * W), F32), shape((T, 2 * W), F32),
            shape((NH, T), F32), shape((W, C), F32),
            shape((1, NH), F32), shape((1, NH), F32), shape((1, C), F32),
        ),
        in_specs=[vmem] * 8,
        out_specs=[anywhere] * 6 + [vmem] * 3,
        scratch_shapes=[S((6,))],
    )(*[pltpu.with_memory_space_constraint(p, pltpu.VMEM) for p in parts])
    return (
        gi[None], gg[None], gk[None], gq[None], gs[None],
        rate.reshape(NH), skip.reshape(NH), norm.reshape(C), gw,
    )


def solution(mesh):
    return jax.shard_map(
        body,
        mesh=mesh,
        in_specs=(
            P("dp", "context", "tensor"),
            P("dp", "context", "tensor"),
            P("dp", "context", "tensor"),
            P("dp", "context", "tensor"),
            P("dp", "tensor", "context"),
            P("tensor"),
            P("tensor"),
            P("tensor"),
            P(None, "tensor"),
            P("dp", "context", "tensor"),
        ),
        out_specs=(
            P("dp", "context", "tensor"),
            P("dp", "context", "tensor"),
            P("dp", "context", "tensor"),
            P("dp", "context", "tensor"),
            P("dp", "tensor", "context"),
            P("tensor"),
            P("tensor"),
            P("tensor"),
            P(("dp", "context"), "tensor"),
        ),
        check_vma=False,
    )
```

```python
import jax
import jax.numpy as jnp
from jax import lax
from jax.experimental import pallas as pl
from jax.experimental.pallas import tpu as pltpu
from jax.sharding import PartitionSpec as P

F32 = jnp.float32
BF = jnp.bfloat16
EPSILON = 1e-05
MESH = pl.DeviceIdType.MESH

T = 256
C = 1024
NH = 16
NQ = 8
W = 128
CTX = 16
FAR_FIRST = sorted(
    [(dx, dz) for dx in range(4) for dz in range(4) if dx or dz],
    key=lambda d: -min(d[0], 4 - d[0]) - min(d[1], 4 - d[1]),
)


def dot(a, b):
    return lax.dot_general(a, b, (((1,), (0,)), ((), ())), preferred_element_type=F32)


def dot_t(a, b):
    return lax.dot_general(a, b, (((1,), (1,)), ((), ())), preferred_element_type=F32)


def tdot(a, b):
    return lax.dot_general(a, b, (((0,), (0,)), ((), ())), preferred_element_type=F32)


def split2(v):
    hi = v.astype(BF)
    return hi, (v - hi.astype(F32)).astype(BF)


def split3(v):
    hi = v.astype(BF)
    rest = v - hi.astype(F32)
    mid = rest.astype(BF)
    return hi, mid, (rest - mid.astype(F32)).astype(BF)


def dot3(v, ones):
    parts = dot(jnp.concatenate(split3(v), axis=0), ones)
    return parts[0:NH] + parts[NH : 2 * NH] + parts[2 * NH : 3 * NH]


def iota(shape, axis):
    return lax.broadcasted_iota(jnp.int32, shape, axis)


def lanes(q):
    return pl.ds(pl.multiple_of(q * W, W), W)


def per_head(row):
    own = (iota((NH, C), 1) // 64) == iota((NH, C), 0)
    return jnp.sum(jnp.where(own, row, 0.0), axis=1, keepdims=True)


def kernel(
    x_hbm, k_hbm, q_hbm, step_hbm, rate_hbm, skip_hbm, gain_hbm, gate_hbm, w_hbm, og_hbm,
    gi_v, gg_v, dk_s, dq_s, gs_v, gw_v, ea_own, la_own,
    x_ref, k_ref, q_ref, step_ref, rate_ref, skip_ref, gain_ref,
    gate_v, w_v, ogf, ogp, ogt, nm2,
    cumx, eexp, wexp, cum_s, stp_s, kt, qt, sc,
    snd, rcv, ent_s, ent, bsnd, brcv, out_s, outb,
    silu_s, bend_s, skx_s, mt, phi, plo, y_s, gn_s, ga_s, g_s, acc, acc2, invb, mub,
    ds_s, dxw, rows, accr, accc, accv,
    ea_rcv, ea_p, la_rcv, la_p, s1, r1, own1, s2, r2,
    in_sem, og_ss, og_rs, leg_ss, leg_rs, ea_ss, ea_rs, p_ss, p_rs, r1_ss, r1_rs, r2_ss, r2_rs,
):
    me = lax.axis_index("context")
    myt = lax.axis_index("tensor")
    mydp = lax.axis_index("dp")
    mz, mx = me // 4, me % 4
    other = 1 - mydp
    right, left = (myt + 1) % 4, (myt + 3) % 4

    barrier = pltpu.get_barrier_semaphore()

    def greet(off, carry):
        pl.semaphore_signal(
            barrier, inc=1, device_id={"context": (me + off) % CTX}, device_id_type=MESH
        )
        return carry

    pl.semaphore_signal(barrier, inc=1, device_id={"tensor": right}, device_id_type=MESH)
    pl.semaphore_signal(barrier, inc=1, device_id={"tensor": left}, device_id_type=MESH)
    lax.fori_loop(1, CTX, greet, 0)
    pl.semaphore_signal(barrier, inc=1, device_id={"dp": other}, device_id_type=MESH)

    loads = [
        pltpu.make_async_copy(src, dst, in_sem.at[i])
        for i, (src, dst) in enumerate(
            (
                (step_hbm, step_ref), (rate_hbm, rate_ref), (skip_hbm, skip_ref), (k_hbm, k_ref),
                (x_hbm, x_ref), (q_hbm, q_ref), (gain_hbm, gain_ref), (og_hbm, ogf.at[myt]),
                (gate_hbm, gate_v), (w_hbm, w_v),
            )
        )
    ]
    for copy in loads:
        copy.start()
    for copy in loads[:3]:
        copy.wait()

    raw = step_ref[...]
    eye = iota((NH, NH), 0) == iota((NH, NH), 1)
    slope = jnp.sum(jnp.where(eye, jnp.exp(rate_ref[...]), 0.0), axis=1, keepdims=True)
    step = jnp.maximum(raw, 0.0) + jnp.log(1.0 + jnp.exp(-jnp.abs(raw)))
    decay = -slope * step
    upper = (iota((T, T), 0) <= iota((T, T), 1)).astype(BF)
    cum = dot3(decay, upper)
    total = cum[:, T - 1 : T]
    stp_s[...] = step
    cum_s[...] = cum
    spread = ((iota((3 * NH, C), 0) % NH) == (iota((3 * NH, C), 1) // 64)).astype(BF)

    def expand(v, to):
        pieces = jnp.concatenate(split3(v), axis=0).astype(F32)
        turned = jnp.concatenate([pieces, jnp.zeros((W - 3 * NH, T), F32)], axis=0).T
        to[...] = dot(turned[:, : 3 * NH].astype(BF), spread)

    expand(jnp.exp(total - cum) * step, wexp)
    expand(jnp.exp(cum), eexp)
    own = (iota((NH, C), 1) // 64) == iota((NH, C), 0)
    skip_col = jnp.sum(jnp.where(eye, skip_ref[...], 0.0), axis=1, keepdims=True)
    rows[3] = jnp.sum(jnp.where(own, skip_col, 0.0), axis=0, keepdims=True)

    loads[3].wait()
    for g in range(2):
        kt[g] = k_ref[:, g * W : (g + 1) * W].T
    loads[4].wait()

    def local_state(q, carry):
        hi, lo = split2(x_ref[:, lanes(q)].astype(F32) * wexp[:, lanes(q)])
        both = dot(kt[q // 4], jnp.concatenate([hi, lo], axis=1))
        state = both[:, :W] + both[:, W:]
        factor = jnp.broadcast_to(eexp[T - 1 : T, lanes(q)], (8, W))
        snd[2 * q, 0:64] = state[0:64]
        snd[2 * q + 1, 0:64] = state[64:]
        snd[2 * q, 64:72] = factor
        snd[2 * q + 1, 64:72] = factor
        return carry

    lax.fori_loop(0, NQ, local_state, 0)

    pl.semaphore_wait(barrier, CTX + 2)

    def send_all(src, dst, leg):
        for dx, dz in FAR_FIRST:
            peer = (mz + dz) % 4 * 4 + (mx + dx) % 4
            pltpu.make_async_remote_copy(
                src_ref=src.at[peer],
                dst_ref=dst.at[me],
                send_sem=leg_ss.at[leg],
                recv_sem=leg_rs.at[leg],
                device_id={"context": peer},
                device_id_type=MESH,
            ).start()

    def all_of(slots, leg):
        some = slots.at[pl.ds(0, CTX - 1)]
        return pltpu.make_async_remote_copy(
            src_ref=some,
            dst_ref=some,
            send_sem=leg_ss.at[leg],
            recv_sem=leg_rs.at[leg],
            device_id={"context": (me + 1) % CTX},
            device_id_type=MESH,
        )

    def ring(src, dst, sem, peer):
        return pltpu.make_async_remote_copy(
            src_ref=src,
            dst_ref=dst,
            send_sem=og_ss.at[0],
            recv_sem=og_rs.at[sem],
            device_id={"tensor": peer},
            device_id_type=MESH,
        )

    top, low = pl.ds(0, 128), pl.ds(128, 128)
    to_right = [ring(og_hbm.at[h], ogf.at[myt, h], i, right) for i, h in enumerate((top, low))]
    to_left = [ring(og_hbm.at[h], ogf.at[myt, h], 2 + i, left) for i, h in enumerate((low, top))]
    to_right[0].start()
    to_left[0].start()
    send_all(snd, rcv, 0)

    to_right[1].start()
    to_left[1].start()

    expand(cum_s[...], cumx)
    loads[5].wait()
    for g in range(2):
        qg = q_ref[:, g * W : (g + 1) * W]
        qt[g] = qg.T
        sc[g] = dot_t(qg, k_ref[:, g * W : (g + 1) * W])
    causal = iota((T, T), 0) >= iota((T, T), 1)
    first = iota((T, W), 1) < 64

    def within(q, carry):
        xp = x_ref[:, lanes(q)]
        spread_tile = cumx[:, lanes(q)]
        outs = []
        for hh in range(2):
            h = 2 * q + hh
            column = spread_tile[:, 64 * hh : 64 * hh + 1]
            gap = column - cum_s[pl.ds(h, 1), :]
            m = jnp.exp(jnp.where(causal, gap, -1e30)) * stp_s[pl.ds(h, 1), :]
            mt[h] = m
            hi, lo = split2(m * sc[q // 4])
            phi[h] = hi
            plo[h] = lo
            outs.append(dot(hi, xp) + dot(lo, xp))
        y_s[:, lanes(q)] = jnp.where(first, outs[0], outs[1])
        return carry

    lax.fori_loop(0, NQ, within, 0)

    rcv[me] = snd[me]
    all_of(rcv, 0).wait_recv()
    run = jnp.zeros((64, W), F32)
    for s in range(CTX):
        ent_s[s] = run
        run = rcv[s, 64:65] * run + rcv[s, 0:64]
    send_all(ent_s, ent, 1)
    ent[me] = ent_s[me]

    to_right[0].wait_recv()
    relay_right = ring(ogf.at[left, top], ogf.at[left, top], 4, right)
    relay_right.start()
    to_left[0].wait_recv()
    relay_left = ring(ogf.at[right, low], ogf.at[right, low], 4, left)
    relay_left.start()
    loads[8].wait()

    def gates(q, carry):
        gate = gate_v[:, lanes(q)].astype(F32)
        sig = 1.0 / (1.0 + jnp.exp(-gate))
        silu = gate * sig
        silu_s[:, lanes(q)] = silu
        bend_s[:, lanes(q)] = sig * (1.0 + gate - silu)
        skx_s[:, lanes(q)] = rows[3, :, lanes(q)] * x_ref[:, lanes(q)].astype(F32)
        return carry

    lax.fori_loop(0, NQ, gates, 0)

    loads[7].wait()
    loads[9].wait()

    def pair(src, dst, sem):
        return pltpu.make_async_remote_copy(
            src_ref=src,
            dst_ref=dst,
            send_sem=p_ss.at[sem],
            recv_sem=p_rs.at[sem],
            device_id={"dp": other},
            device_id_type=MESH,
        )

    def pair_og(chunk):
        return pair(ogf.at[chunk], ogp.at[chunk % 2], chunk % 2)

    def hand_over(chunk):
        @pl.when(chunk // 2 == other)
        def _():
            pair_og(chunk).start()

        @pl.when(chunk // 2 == mydp)
        def _():
            def turn(i, carry):
                at = pl.ds(pl.multiple_of((chunk % 2) * C + i * W, W), W)
                ogt[at, 0:T] = ogf[chunk, :, lanes(i)].T
                return carry

            lax.fori_loop(0, 8, turn, 0)

    def project(chunk, first_term):
        def one(n, carry):
            where = pl.ds(pl.multiple_of(n * 256, 256), 256)
            part = dot(ogf[chunk], w_v[pl.ds(pl.multiple_of(chunk * C, C), C), where])
            gn_s[:, where] = part if first_term else gn_s[:, where] + part
            return carry

        lax.fori_loop(0, 4, one, 0)

    def take(chunk, first_term):
        hand_over(chunk)
        project(chunk, first_term)

    def turn_pair(chunk):
        @pl.when(chunk // 2 == mydp)
        def _():
            pair_og(chunk).wait_recv()

            def turn(i, carry):
                at = pl.ds(pl.multiple_of((chunk % 2) * C + i * W, W), W)
                ogt[at, T : 2 * T] = ogp[chunk % 2, :, lanes(i)].T
                return carry

            lax.fori_loop(0, 8, turn, 0)

    take(myt, True)
    loads[6].wait()
    to_right[1].wait_recv()
    to_left[1].wait_recv()
    hand_over(left)
    hand_over(right)
    turn_pair(myt)
    project(left, False)
    turn_pair(left)
    turn_pair(right)
    all_of(ent, 1).wait_recv()

    acc[...] = jnp.zeros_like(acc)

    def entering(q):
        return jnp.concatenate([ent[2 * q], ent[2 * q + 1]], axis=0)

    def group_q(q):
        return q_ref[:, lanes(q // 4)]

    def scan_out(q, carry):
        g = q // 4
        twice = jnp.concatenate([group_q(q), group_q(q)], axis=1)
        carried = dot(twice, jnp.concatenate(split2(entering(q)), axis=0))
        y = y_s[:, lanes(q)] + eexp[:, lanes(q)] * carried
        y_s[:, lanes(q)] = y
        gated = (y + skx_s[:, lanes(q)]) * silu_s[:, lanes(q)]
        ga_s[:, lanes(q)] = gated
        acc[g] += gated * gated
        return carry

    lax.fori_loop(0, NQ, scan_out, 0)
    for g in range(2):
        mean = jnp.sum(acc[g], axis=1, keepdims=True) * (1.0 / 512)
        invb[g] = jnp.broadcast_to(lax.rsqrt(mean + EPSILON), (T, W))

    def normalize(q, carry):
        value = ga_s[:, lanes(q)] * invb[q // 4] * gain_ref[:, lanes(q)]
        nm2[0:T, lanes(q)] = value.astype(BF)
        return carry

    lax.fori_loop(0, NQ, normalize, 0)
    pair_nm = pair(nm2.at[0:T], nm2.at[T : 2 * T], 2)
    pair_nm.start()

    ring(ogf.at[0], ogf.at[0], 4, right).wait_recv()
    hand_over((myt + 2) % 4)
    project(right, False)
    turn_pair((myt + 2) % 4)
    pair_nm.wait_recv()

    def ahead(v):
        return (v + 1 + 2 * mydp) % 4

    def behind(v):
        return (v + 3 - 2 * mydp) % 4

    def far(v):
        return (v + 2) % 4

    def along(phase, half, v):
        return mz * 4 + v if phase == half else v * 4 + mx

    def mine(phase, half):
        return mx if phase == half else mz

    def place(half, j):
        v = mine(1, half)
        return (far(v), ahead(v), behind(v), v)[j]

    def weight(half, v, to, slot):
        def block(j):
            i = place(half, j)
            return (i * 4 + v) if half == 0 else (v * 4 + i)

        left_side = jnp.concatenate(
            [ogt[pl.ds(pl.multiple_of(block(i) * W, W), W), :] for i in range(4)], axis=0
        )

        def one(n, carry):
            at = pl.ds(pl.multiple_of(half * 512 + n * 256, 256), 256)
            value = dot(left_side, nm2[:, at])
            for i in range(4):
                to[slot, i, :, pl.ds(pl.multiple_of(n * 256, 256), 256)] = value[
                    i * W : (i + 1) * W
                ].astype(to.dtype)
            return carry

        lax.fori_loop(0, 2, one, 0)

    def phase1(slot, peer, part):
        at = pl.ds(2 * part, 2)
        return pltpu.make_async_remote_copy(
            src_ref=s1.at[slot, at],
            dst_ref=r1.at[slot, at],
            send_sem=r1_ss.at[0],
            recv_sem=r1_rs.at[part if slot > 1 else 2 + 2 * slot + part],
            device_id={"context": peer},
            device_id_type=MESH,
        )

    def phase2(slot, peer):
        return pltpu.make_async_remote_copy(
            src_ref=s2.at[slot],
            dst_ref=r2.at[slot],
            send_sem=r2_ss.at[0],
            recv_sem=r2_rs.at[0],
            device_id={"context": peer},
            device_id_type=MESH,
        )

    def start1(slot, peer, part):
        phase1(slot, peer, part).start()

    def start2(slot, peer):
        phase2(slot, peer).start()

    def every1(ref, sem):
        return pltpu.make_async_remote_copy(
            src_ref=s1,
            dst_ref=ref,
            send_sem=r1_ss.at[0],
            recv_sem=r1_rs.at[sem],
            device_id={"context": (me + 1) % CTX},
            device_id_type=MESH,
        )

    every2 = pltpu.make_async_remote_copy(
        src_ref=s2,
        dst_ref=r2,
        send_sem=r2_ss.at[0],
        recv_sem=r2_rs.at[0],
        device_id={"context": (me + 1) % CTX},
        device_id_type=MESH,
    )

    for half in range(2):
        v = mine(0, half)
        weight(half, far(v), s1, half)
        for part in range(2):
            start1(half, along(0, half, ahead(v)), part)

    project((myt + 2) % 4, False)
    acc2[...] = jnp.zeros_like(acc2)

    def norm_sums(q, carry):
        acc2[q // 4] += gn_s[:, lanes(q)] * gain_ref[:, lanes(q)] * ga_s[:, lanes(q)]
        return carry

    lax.fori_loop(0, NQ, norm_sums, 0)
    for g in range(2):
        inverse = invb[g]
        shift = jnp.sum(acc2[g], axis=1, keepdims=True) * (1.0 / 512)
        mub[g] = shift * inverse * inverse

    def norm_back(q, carry):
        g = q // 4
        gated = ga_s[:, lanes(q)]
        inverse = invb[g]
        gn = gn_s[:, lanes(q)]
        d_gated = inverse * (gn * gain_ref[:, lanes(q)] - gated * mub[g])
        rows[0, :, lanes(q)] = jnp.sum(gn * gated * inverse, axis=0, keepdims=True)
        xv = x_ref[:, lanes(q)].astype(F32)
        ssd = y_s[:, lanes(q)] + skx_s[:, lanes(q)]
        gg_v[:, lanes(q)] = (d_gated * ssd * bend_s[:, lanes(q)]).astype(BF)
        grad = d_gated * silu_s[:, lanes(q)]
        g_s[:, lanes(q)] = grad
        rows[1, :, lanes(q)] = jnp.sum(grad * xv, axis=0, keepdims=True)
        hi, lo = split2(eexp[:, lanes(q)] * grad)
        both = dot(qt[g], jnp.concatenate([hi, lo], axis=1))
        into = (both[:, :W] + both[:, W:]).astype(BF)
        bsnd[2 * q] = into[0:64]
        bsnd[2 * q + 1] = into[64:]
        return carry

    lax.fori_loop(0, NQ, norm_back, 0)
    send_all(bsnd, brcv, 2)

    for half in range(2):
        weight(half, behind(mine(0, half)), s1, 2 + half)

    def send_behind(part):
        for half in range(2):
            start1(2 + half, along(0, half, behind(mine(0, half))), part)

    def relay1(part):
        for half in range(2):
            phase1(half, me, part).wait_recv()
            for i in (2 * part, 2 * part + 1):
                s1[4 + half, i] = (own1[2 + half, i] + r1[half, i].astype(F32)).astype(BF)
            start1(4 + half, along(0, half, ahead(mine(0, half))), part)

    for half in range(2):
        weight(half, ahead(mine(0, half)), own1, 2 + half)
    for half in range(2):
        weight(half, mine(0, half), own1, half)
    send_behind(0)
    relay1(0)
    brcv[me] = bsnd[me]
    all_of(brcv, 2).wait_recv()
    run = jnp.zeros((64, W), F32)
    for s in range(CTX - 1, -1, -1):
        out_s[s] = run.astype(BF)
        run = brcv[s].astype(F32) + rcv[s, 64:65] * run
    send_all(out_s, outb, 3)
    outb[me] = out_s[me]

    ds_s[...] = jnp.zeros_like(ds_s)
    dq_s[...] = jnp.zeros_like(dq_s)
    accr[...] = jnp.zeros_like(accr)
    accc[...] = jnp.zeros_like(accc)
    accv[...] = jnp.zeros_like(accv)

    def head_sums(q, value):
        row, lane = iota((NH, 2 * W), 0), iota((NH, 2 * W), 1) % W
        pick = (row == 2 * q + lane // 64).astype(BF)
        return dot_t(pick, jnp.concatenate(split2(value), axis=1))

    def within_back(q, carry):
        g = q // 4
        xp = x_ref[:, lanes(q)]
        grad = g_s[:, lanes(q)]
        ghi, glo = split2(grad)
        gthi, gtlo = ghi.T, glo.T
        x2 = jnp.concatenate([xp, xp], axis=1)
        zero = jnp.zeros((T, W), BF)
        parts = []
        total_ds = ds_s[g]
        for hh in range(2):
            h = 2 * q + hh
            keep = first if hh == 0 else jnp.logical_not(first)
            g2 = jnp.concatenate([jnp.where(keep, ghi, zero), jnp.where(keep, glo, zero)], axis=1)
            total_ds = total_ds + dot_t(g2, x2) * mt[h]
            a, b = gthi[64 * hh : 64 * hh + 64], gtlo[64 * hh : 64 * hh + 64]
            both = dot(jnp.concatenate([a, b], axis=0), phi[h])
            parts.append(both[0:64] + both[64:] + dot(a, plo[h]))
        ds_s[g] = total_ds
        dxw[:, lanes(q)] = jnp.concatenate(parts, axis=0).T
        accr[...] += head_sums(q, grad * y_s[:, lanes(q)])
        ehi, elo = split2(eexp[:, lanes(q)] * grad)
        shi, slo = split2(entering(q))
        to_q = dot_t(jnp.concatenate([ehi, elo], axis=1), jnp.concatenate([shi, shi], axis=1))
        dq_s[:, lanes(g)] += to_q + dot_t(ehi, slo)
        return carry

    lax.fori_loop(0, NQ, within_back, 0)
    send_behind(1)
    relay1(1)
    for g in range(2):
        hi, lo = split2(ds_s[g])
        kg = k_ref[:, g * W : (g + 1) * W]
        qg = q_ref[:, g * W : (g + 1) * W]
        dq_s[:, g * W : (g + 1) * W] += dot(hi, kg) + dot(lo, kg)
        dk_s[:, g * W : (g + 1) * W] = tdot(hi, qg) + tdot(lo, qg)

    def row_send(src, dst, leg):
        def one(off, carry):
            peer = (me + off) % CTX
            pltpu.make_async_remote_copy(
                src_ref=src,
                dst_ref=dst.at[me],
                send_sem=leg_ss.at[leg],
                recv_sem=leg_rs.at[leg],
                device_id={"context": peer},
                device_id_type=MESH,
            ).start()
            return carry

        lax.fori_loop(1, CTX, one, 0)
        dst[me] = src[...]

    def row_sum(src, dst, leg):
        all_of(dst, leg).wait_recv()
        value = dst[0]
        for i in range(1, CTX):
            value = value + dst[i]
        all_of(dst, leg).wait_send()
        src[...] = value

    def line_send(stage):
        spot = mz if stage else mx
        for d in (2, 1, 3):
            there = (spot + d) % 4
            pltpu.make_async_remote_copy(
                src_ref=ea_rcv.at[stage, spot],
                dst_ref=ea_rcv.at[stage, spot],
                send_sem=ea_ss.at[stage],
                recv_sem=ea_rs.at[stage],
                device_id={"context": there * 4 + mx if stage else mz * 4 + there},
                device_id_type=MESH,
            ).start()

    def line_sum(stage):
        some = ea_rcv.at[stage, pl.ds(0, 3)]
        whole = pltpu.make_async_remote_copy(
            src_ref=some,
            dst_ref=some,
            send_sem=ea_ss.at[stage],
            recv_sem=ea_rs.at[stage],
            device_id={"context": (me + 1) % CTX},
            device_id_type=MESH,
        )
        whole.wait_recv()
        whole.wait_send()
        return ea_rcv[stage, 0] + ea_rcv[stage, 1] + ea_rcv[stage, 2] + ea_rcv[stage, 3]

    def as_row(column):
        at = iota((NH, W), 0) == iota((NH, W), 1)
        return jnp.sum(jnp.where(at, column, 0.0), axis=0, keepdims=True)

    ea_own[:, 0:C] = rows[0]
    ea_own[:, C : C + W] = as_row(per_head(rows[1]))
    ea_rcv[0, mx] = ea_own[...]
    line_send(0)

    all_of(outb, 3).wait_recv()

    def state_back(q, carry):
        g = q // 4
        d_state = jnp.concatenate([outb[2 * q], outb[2 * q + 1]], axis=0)
        rows[2, :, lanes(q)] = jnp.sum(
            d_state.astype(F32) * entering(q), axis=0, keepdims=True
        )
        weights = wexp[:, lanes(q)]
        xv = x_ref[:, lanes(q)].astype(F32)
        via = weights * dot(k_ref[:, lanes(g)], d_state)
        dx = dxw[:, lanes(q)] + via
        gi_v[:, lanes(q)] = (dx + rows[3, :, lanes(q)] * g_s[:, lanes(q)]).astype(BF)
        accc[...] += head_sums(q, xv * dx)
        accv[...] += head_sums(q, xv * via)
        whi, wlo = split2(weights * xv)
        twice = jnp.concatenate([d_state, d_state], axis=1)
        dk_s[:, lanes(g)] += dot_t(jnp.concatenate([whi, wlo], axis=1), twice)
        return carry

    lax.fori_loop(0, NQ, state_back, 0)

    raw = step_ref[...]
    slope = jnp.sum(jnp.where(eye, jnp.exp(rate_ref[...]), 0.0), axis=1, keepdims=True)
    step = stp_s[...]
    lower = (iota((T, T), 0) >= iota((T, T), 1)).astype(BF)
    after = dot3(accr[...] - accc[...], lower)
    log_grad = per_head(rows[2] * eexp[T - 1 : T, :])
    d_total = jnp.sum(accv[...], axis=1, keepdims=True) + log_grad
    d_decay = after + d_total
    gs_v[...] = (accc[...] / step - slope * d_decay) / (1.0 + jnp.exp(-raw))
    la_own[...] = as_row(jnp.sum(d_decay * (-slope * step), axis=1, keepdims=True))
    row_send(la_own, la_rcv, 5)

    def await1(part):
        every1(r1.at[pl.ds(2, 4), pl.ds(2 * part, 2)], part).wait_recv()

    def summed(half, j):
        return own1[half, j] + r1[2 + half, j].astype(F32) + r1[4 + half, j].astype(F32)

    await1(0)
    for half in range(2):
        v = mine(1, half)
        for j, there in ((0, far(v)), (1, ahead(v))):
            s2[2 * j + half] = summed(half, j).astype(BF)
            start2(2 * j + half, along(1, half, there))

    await1(1)
    for half in range(2):
        s2[4 + half] = summed(half, 2).astype(BF)
        start2(4 + half, along(1, half, behind(mine(1, half))))
    for half in range(2):
        gw_v[:, half * 512 : half * 512 + 512] = summed(half, 3)

    ea_rcv[1, mz] = line_sum(0)
    line_send(1)
    row_sum(la_own, la_rcv, 5)
    pair_la = pair(la_own, la_p, 4)
    pair_la.start()
    ea_own[...] = line_sum(1)
    pair_ea = pair(ea_own, ea_p, 3)
    pair_ea.start()
    all_of(rcv, 0).wait_send()
    all_of(ent, 1).wait_send()
    all_of(brcv, 2).wait_send()
    all_of(outb, 3).wait_send()

    pair_ea.wait()
    ea_own[...] += ea_p[...]
    pair_la.wait()
    la_own[...] += la_p[...]
    ring(ogf.at[pl.ds(0, 3)], ogf.at[pl.ds(0, 3)], 4, right).wait_send()
    pair_nm.wait_send()
    every1(r1, 0).wait_send()
    for i in range(2):
        pair_og(2 * other + i).wait_send()
    every2.wait_recv()
    for half in range(2):
        at = slice(half * 512, half * 512 + 512)
        gw_v[:, at] += (
            r2[half].astype(F32) + r2[2 + half].astype(F32) + r2[4 + half].astype(F32)
        )
    every2.wait_send()


def hand_out(
    gi_v, gg_v, gk_v, gq_v, gs_v, gw_v, early_v, late_v,
    gi_out, gg_out, gk_out, gq_out, gs_out, gw_out, rate_ref, skip_ref, norm_ref, out_sem,
):
    ways = (
        (gi_v, gi_out), (gg_v, gg_out), (gw_v, gw_out), (gk_v, gk_out), (gq_v, gq_out),
        (gs_v, gs_out),
    )
    out = [pltpu.make_async_copy(*way, out_sem.at[i]) for i, way in enumerate(ways)]
    for copy in out:
        copy.start()
    norm_ref[...] = early_v[:, 0:C]
    skip_ref[...] = early_v[:, C : C + NH]
    rate_ref[...] = late_v[:, 0:NH]
    for copy in out:
        copy.wait()


def body(
    ssm_input, gate_input, state_keys, state_queries, step_raw,
    rate_log, skip_gain, norm_gain, out_weight, out_grad,
):
    vmem, anywhere = pl.BlockSpec(memory_space=pltpu.VMEM), pl.BlockSpec(memory_space=pl.ANY)
    V, S = pltpu.VMEM, pltpu.SemaphoreType.DMA
    shape = jax.ShapeDtypeStruct
    wide, by_pos, per_ctx = V((T, C), F32), V((2, T, W), F32), V((CTX, 64, W), BF)
    scratch = [
        V((T, C), BF), V((T, 2 * W), BF), V((T, 2 * W), BF), V((NH, T), F32), V((1, NH), F32),
        V((1, NH), F32), V((1, C), F32),
        V((T, C), BF), V((4 * C, C), BF), V((4, T, C), BF), V((2, T, C), BF), V((2 * C, 2 * T), BF),
        V((2 * T, C), BF),
        wide, wide, wide, V((NH, T), F32), V((NH, T), F32), V((2, W, T), BF), V((2, W, T), BF),
        V((2, T, T), F32),
        V((CTX, 72, W), F32), V((CTX, 72, W), F32), V((CTX, 64, W), F32), V((CTX, 64, W), F32),
        per_ctx, per_ctx, per_ctx, per_ctx,
        wide, wide, wide, V((NH, T, T), F32), V((NH, T, T), BF), V((NH, T, T), BF),
        wide, wide, wide, wide, by_pos, by_pos, by_pos, by_pos,
        V((2, T, T), F32), wide,
        V((4, 1, C), F32), V((NH, T), F32), V((NH, T), F32), V((NH, T), F32),
        V((2, 4, 1, C + W), F32), V((1, C + W), F32), V((CTX, 1, W), F32), V((1, W), F32),
        V((6, 4, W, 512), BF), V((6, 4, W, 512), BF), V((4, 4, W, 512), F32),
        V((6, W, 512), BF), V((6, W, 512), BF),
        S((10,)), S((1,)), S((5,)), S((6,)), S((6,)), S((2,)), S((2,)),
        S((5,)), S((5,)), S((1,)), S((6,)), S((1,)), S((1,)),
    ]
    parts = pl.pallas_call(
        kernel,
        out_shape=(
            V((T, C), BF), V((T, C), BF), V((T, 2 * W), F32), V((T, 2 * W), F32),
            V((NH, T), F32), V((W, C), F32), V((1, C + W), F32), V((1, W), F32),
        ),
        in_specs=[anywhere] * 10,
        out_specs=[vmem] * 8,
        scratch_shapes=scratch,
        compiler_params=pltpu.CompilerParams(
            collective_id=0, has_side_effects=True, vmem_limit_bytes=60 * 1024 * 1024
        ),
    )(
        ssm_input[0], state_keys[0], state_queries[0], step_raw[0],
        rate_log.reshape(1, NH), skip_gain.reshape(1, NH), norm_gain.reshape(1, C),
        gate_input[0], out_weight, out_grad[0],
    )
    gi, gg, gk, gq, gs, gw, rate, skip, norm = pl.pallas_call(
        hand_out,
        out_shape=(
            shape((T, C), BF), shape((T, C), BF), shape((T, 2 * W), F32), shape((T, 2 * W), F32),
            shape((NH, T), F32), shape((W, C), F32),
            shape((1, NH), F32), shape((1, NH), F32), shape((1, C), F32),
        ),
        in_specs=[vmem] * 8,
        out_specs=[anywhere] * 6 + [vmem] * 3,
        scratch_shapes=[S((6,))],
    )(*[pltpu.with_memory_space_constraint(p, pltpu.VMEM) for p in parts])
    return (
        gi[None], gg[None], gk[None], gq[None], gs[None],
        rate.reshape(NH), skip.reshape(NH), norm.reshape(C), gw,
    )


def solution(mesh):
    return jax.shard_map(
        body,
        mesh=mesh,
        in_specs=(
            P("dp", "context", "tensor"),
            P("dp", "context", "tensor"),
            P("dp", "context", "tensor"),
            P("dp", "context", "tensor"),
            P("dp", "tensor", "context"),
            P("tensor"),
            P("tensor"),
            P("tensor"),
            P(None, "tensor"),
            P("dp", "context", "tensor"),
        ),
        out_specs=(
            P("dp", "context", "tensor"),
            P("dp", "context", "tensor"),
            P("dp", "context", "tensor"),
            P("dp", "context", "tensor"),
            P("dp", "tensor", "context"),
            P("tensor"),
            P("tensor"),
            P("tensor"),
            P(("dp", "context"), "tensor"),
        ),
        check_vma=False,
    )
```
